128 devices in a mesh: row: 8 (over x, core), col: 16 (over z, y).
Axes of the slice: x: 4, y: 4, z: 4, core: 2. Of those that a mesh axis runs over, the one named last changes fastest.
Arguments:
- currents: bfloat16 [49152, 256], P(('row', 'col')), may hold values from -6 to 6
- incidence: int32 [2, 49152], P(None, ('row', 'col')), may hold values from 0 to 32767, as said below
- centroids: int32 [3, 32768], P(None, ('row', 'col')), may hold values from 0 to 255, as said below
- sweep_weights: float32 [2], replicated, may hold values from 0.2 to 0.6
Outputs:
- updated: bfloat16 [49152, 256], P(('row', 'col'))
- potentials: bfloat16 [32768, 256], P(('row', 'col'))
The draws below stay inside these ranges and needn't reach their ends.
Inputs may be any that keep to these rules, and one draw needn't show every extreme that they name: `incidence`: triangles o * 256 to (o + 1) * 256 - 1 form owner block o. Counting both rows, the edges of one device name at most 16 triangles of any one owner block, and exactly 16 of some block on every device. `centroids`: first two rows from 0 to 255, third row from 0 to 3.
All inputs are finite; a program needn't handle non-finite values.
Results may differ from the reference program's by a relative error of at most 0.006.
Values may be sent and summed in bfloat16 or wider, within the bound.
A program may use at most 128 MiB of HBM per device.

```python
import math
import jax
import jax.numpy as jnp
from jax import lax

TRI_DEV = 256
EXC = 128
SWEEPS = 2
GRID = 256
DEPTH = 4
EDGE_DEV = 384
CAP = 16
TRIANGLES = 32768
EDGES = 49152
DEVICES = 128


def draw_incidence(key, part):
    cells = DEVICES * CAP
    contributions = 2 * EDGE_DEV
    n_hot = max(1, DEVICES // 16)
    hot_order = jax.random.permutation(jax.random.fold_in(key, 11), DEVICES)
    hot_flag = jnp.zeros((DEVICES,), jnp.int32).at[hot_order[:n_hot]].set(1)
    owner_of_cell = jnp.arange(cells, dtype=jnp.int32) // CAP
    spread = max(1, 2 ** 28 // cells)

    def one_device(device_key):
        key_full, key_base, key_perm, key_local = jax.random.split(device_key, 4)
        full_owner = jax.random.randint(key_full, (), 0, DEVICES)
        base = jax.random.randint(key_base, (cells,), 0, spread) * cells + jnp.arange(cells, dtype=jnp.int32)
        score = base + hot_flag[owner_of_cell] * 2 ** 28 + (owner_of_cell == full_owner).astype(jnp.int32) * 2 ** 29
        _, chosen = lax.top_k(score, contributions)
        order = jax.random.permutation(key_perm, contributions)
        chosen = chosen[order]
        local = jax.random.randint(key_local, (contributions,), 0, TRI_DEV)
        triangle = chosen // CAP * TRI_DEV + local
        return triangle.reshape(2, EDGE_DEV)
    device_keys = jax.random.split(jax.random.fold_in(key, 5), DEVICES)
    per_device = jax.vmap(one_device)(device_keys)
    return jnp.transpose(per_device, (1, 0, 2)).reshape(2, DEVICES * EDGE_DEV).astype(jnp.int32)


def draw_centroids(key, part):
    key_x, key_y, key_z = jax.random.split(jax.random.fold_in(key, 3), 3)
    first = jax.random.randint(key_x, (TRIANGLES,), 0, GRID)
    second = jax.random.randint(key_y, (TRIANGLES,), 0, GRID)
    third = jax.random.randint(key_z, (TRIANGLES,), 0, DEPTH)
    return jnp.stack([first, second, third]).astype(jnp.int32)


def level_of(stream_key, extent, cuts, smallest, top_value):
    def one(position, shards_of):
        draws = jax.random.uniform(jax.random.fold_in(jax.random.fold_in(stream_key, 6), position), (shards_of,), jnp.float32, smallest / len(cuts), top_value / len(cuts))
        return jnp.repeat(jnp.exp(draws), extent[position] // shards_of).reshape((-1,) + (1,) * (len(extent) - position - 1))

    factor_of = one(*cuts[0])
    for cut in cuts[1:]:
        factor_of = factor_of * one(*cut)
    return factor_of


def scatter_about(rng, extent, width, limit, shards=(), held_as=jnp.bfloat16):
    level = level_of(rng, extent, shards, -0.22, 0.18) if shards else 1.0
    entries = jax.random.normal(rng, extent, jnp.float32) * width * level
    return jnp.minimum(jnp.maximum(entries, -limit), limit).astype(held_as)


def setup_inputs(seed: int = 0) -> dict:
    arg_keys = jax.random.split(jax.random.key(seed), 5)
    currents = scatter_about(arg_keys[0], (EDGES, 2 * EXC), 1.0, 6.0, ((0, 128),))
    incidence = draw_incidence(jax.random.fold_in(arg_keys[4], 71), 0)
    centroids = draw_centroids(jax.random.fold_in(arg_keys[4], 71), 0)
    sweep_weights = jnp.clip(jnp.exp(jax.random.uniform(arg_keys[3], (SWEEPS,), jnp.float32, math.log(0.2), math.log(0.6))), 0.2, 0.6)
    return {"currents": currents, "incidence": incidence, "centroids": centroids, "sweep_weights": sweep_weights}


WAVE = 0.19634954084936207
SOFT = 1.0
SPACING = 0.2

def tile_pair(row_pts, col_pts):
    dx = (row_pts[0][:, None] - col_pts[0][None, :]).astype(jnp.float32)
    dy = (row_pts[1][:, None] - col_pts[1][None, :]).astype(jnp.float32)
    dz = (row_pts[2][:, None] - col_pts[2][None, :]).astype(jnp.float32)
    radius = jnp.sqrt(dx * dx + dy * dy + dz * dz + SOFT * SOFT)
    scaled = SPACING / radius
    return ((scaled * jnp.cos(WAVE * radius)).astype(jnp.bfloat16), (-scaled * jnp.sin(WAVE * radius)).astype(jnp.bfloat16))

def blend(real_part, imag_part):
    half = real_part.shape[1] // 2
    return jnp.concatenate([real_part[:, :half] - imag_part[:, half:], real_part[:, half:] + imag_part[:, :half]], 1)

def potentials_of(charges, centroids):
    total = centroids.shape[1]
    block = min(512, total)

    def one_block(index):
        points = lax.dynamic_slice_in_dim(centroids, index * block, block, 1)
        g_real, g_imag = tile_pair(points, centroids)
        return blend(jnp.dot(g_real, charges, preferred_element_type=jnp.float32), jnp.dot(g_imag, charges, preferred_element_type=jnp.float32))
    blocks = lax.map(one_block, jnp.arange(total // block, dtype=jnp.int32))
    return blocks.reshape(total, charges.shape[1])

def reference(currents, incidence, centroids, sweep_weights):
    total = centroids.shape[1]
    current = currents
    potential = None
    for sweep in range(SWEEPS):
        flow = current.astype(jnp.float32)
        charges = jnp.zeros((total, flow.shape[1]), jnp.float32)
        charges = charges.at[incidence[0]].add(flow).at[incidence[1]].add(-flow)
        charges = charges.astype(jnp.bfloat16)
        potential = potentials_of(charges, centroids).astype(jnp.bfloat16)
        slope = potential[incidence[0]].astype(jnp.float32) - potential[incidence[1]].astype(jnp.float32)
        current = (flow - sweep_weights[sweep] * slope).astype(jnp.bfloat16)
    return (current, potential)
```

```python
import functools

import jax
import jax.numpy as jnp
from jax import lax
from jax.experimental import pallas as pl
from jax.experimental.pallas import tpu as pltpu
from jax.sharding import PartitionSpec as P

MESH = pl.DeviceIdType.MESH
F32 = jnp.float32
BF16 = jnp.bfloat16

COS = (0.9999992, -19.73897818, 64.92858784, -85.27084363, 58.78694076, -21.06542941)
SIN = (6.28318491, -41.3415883, 81.59991362, -76.6141403, 41.34136538, -12.46881862)
AMP = 0.2 / 32.0


def iota(shape, dim):
    return lax.broadcasted_iota(jnp.int32, shape, dim)


def horner(coefs, s, scale):
    acc = jnp.float32(coefs[-1] * scale)
    for c in coefs[-2::-1]:
        acc = acc * s + jnp.float32(c * scale)
    return acc


def features(points, as_rows):
    n = points.shape[1]
    x, y, z = points[0:1], points[1:2], points[2:3]
    norm = x * x + y * y + z * z
    if as_rows:
        norm = norm + 1
    top = norm - (norm & 511)
    low = norm & 511
    mid = low - (low & 1)
    bit = low & 1
    one = jnp.ones((1, n), jnp.int32)
    if as_rows:
        rows = [x, y, z, top, mid, bit, one, one, one]
        scale = 1.0
    else:
        rows = [-2 * x, -2 * y, -2 * z, one, one, one, top, mid, bit]
        scale = 1.0 / 1024.0
    at = iota((16, n), 0)
    out = jnp.zeros((16, n), F32)
    for k, row in enumerate(rows):
        out = jnp.where(at == k, row.astype(F32) * scale, out)
    return out.astype(BF16)


def kernel(
    n_row, n_col,
    cur_ref, inc_ref, cen_ref, w_ref,
    upd_ref, pot_ref,
    tile, b_out, b_in, f_out, f_in, q_in, rs_out, rs_in, qq, place, pick,
    lab_flat, lab_out, lab_in, row_cen, col_cen, feat_row, feat_col, cur,
    send_sem, recv_sem,
):
    devices = n_row * n_col
    edge_dev, width = cur_ref.shape
    half = width // 2
    tri = cen_ref.shape[1]
    cells = b_out.shape[0]
    slots = cells // devices
    n_cols = n_row * tri
    n_sweeps = w_ref.shape[0]
    my_row, my_col = lax.axis_index("row"), lax.axis_index("col")
    me = my_row * n_col + my_col

    def flat_id(index):
        return (lax.div(index, n_col), lax.rem(index, n_col))

    def ahead(d):
        return flat_id(lax.rem(me + d, devices))

    def behind(d):
        return flat_id(lax.rem(me + devices - d, devices))

    def row_ahead(r):
        return (lax.rem(my_row + r, n_row), my_col)

    def col_ahead(t):
        return (my_row, lax.rem(my_col + t, n_col))

    def remote(src, dst, k, device):
        return pltpu.make_async_remote_copy(
            src_ref=src, dst_ref=dst, send_sem=send_sem.at[k], recv_sem=recv_sem.at[k],
            device_id=device, device_id_type=MESH,
        )

    barrier = pltpu.get_barrier_semaphore()

    def greet(d, carry):
        pl.semaphore_signal(barrier, inc=1, device_id=ahead(d), device_id_type=MESH)
        return carry

    lax.fori_loop(1, devices, greet, 0)

    both = jnp.concatenate([inc_ref[0:1, :], inc_ref[1:2, :]], axis=1)
    n_con = both.shape[1]
    owner = lax.shift_right_logical(both, tri.bit_length() - 1)
    local = (both & (tri - 1)).astype(F32)
    rel = (owner - me + devices) & (devices - 1)
    hits = jnp.where(rel == iota((devices, n_con), 0), 1.0, 0.0)
    hits16 = hits.astype(BF16)
    earlier = jnp.where(iota((n_con, n_con), 0) < iota((n_con, n_con), 1), 1.0, 0.0).astype(BF16)
    before = jnp.dot(hits16, earlier, preferred_element_type=F32)
    rank = jnp.sum(hits * before, axis=0, keepdims=True)
    slot = rel.astype(F32) * float(slots) + rank
    marks = jnp.where(rank == iota((128, n_con), 0).astype(F32), local + 1.0, 0.0).astype(BF16)
    lab_flat[...] = lax.dot_general(
        hits16, marks, (((1,), (1,)), ((), ())), preferred_element_type=F32
    )
    slot_plus, slot_minus = slot[:, :edge_dev], slot[:, edge_dev:]

    def spread(d, carry):
        lab_out[d] = lab_flat[pl.ds(d, 1), :]
        return carry

    lax.fori_loop(0, devices, spread, 0)
    chunk = 256

    def fill_place(h, carry):
        at = (iota((chunk, edge_dev), 0) + h * chunk).astype(F32)
        rows = jnp.where(slot_plus == at, 1.0, 0.0) - jnp.where(slot_minus == at, 1.0, 0.0)
        place[pl.ds(pl.multiple_of(h * chunk, chunk), chunk), :] = rows.astype(BF16)
        return carry

    lax.fori_loop(0, cells // chunk, fill_place, 0)
    cur[...] = cur_ref[...]

    def fill_out():
        def one(h, carry):
            at = pl.ds(pl.multiple_of(h * chunk, chunk), chunk)
            b_out[at, :] = jnp.dot(place[at, :], cur[...], preferred_element_type=F32).astype(BF16)
            return carry

        lax.fori_loop(0, cells // chunk, one, 0)

    fill_out()
    pl.semaphore_wait(barrier, devices - 1)

    K_ROWC, K_COLC, K_LAB = 0, 1, 2
    K_B, K_Q, K_R, K_F = 3, 3 + n_sweeps, 3 + 2 * n_sweeps, 3 + 3 * n_sweeps

    def send_row_cen(t, carry):
        to = (my_row, lax.rem(my_col + 2 * n_col - 1 - t, n_col))
        remote(cen_ref, row_cen.at[t], K_ROWC, to).start()
        return carry

    def send_col_cen(r, carry):
        remote(cen_ref, col_cen.at[r], K_COLC, row_ahead(r)).start()
        return carry

    lax.fori_loop(0, n_col - 1, send_row_cen, 0)
    lax.fori_loop(1, n_row, send_col_cen, 0)

    def block(d):
        return pl.ds(pl.multiple_of(d * slots, slots), slots)

    def send_labels(d, carry):
        remote(lab_out.at[d], lab_in.at[d], K_LAB, ahead(d)).start()
        return carry

    lax.fori_loop(1, devices, send_labels, 0)

    def send_currents(sweep):
        def one(d, carry):
            remote(b_out.at[block(d)], b_in.at[sweep, block(d)], K_B + sweep, ahead(d)).start()
            return carry

        lax.fori_loop(1, devices, one, 0)

    rest = pl.ds(slots, cells - slots)
    nobody = ahead(1)

    send_currents(0)
    b_in[0, 0:slots, :] = b_out[0:slots, :]
    lab_in[0] = lab_out[0]
    row_cen[n_col - 1] = cen_ref[...]
    col_cen[0] = cen_ref[...]

    drop_rows = pl.ds(0, n_col - 1)
    drop_cols = pl.ds(1, n_row - 1)
    row_wait = remote(row_cen.at[drop_rows], row_cen.at[drop_rows], K_ROWC, nobody)
    col_wait = remote(col_cen.at[drop_cols], col_cen.at[drop_cols], K_COLC, nobody)
    row_wait.wait_send()
    col_wait.wait_send()
    row_wait.wait_recv()
    col_wait.wait_recv()
    for t in range(n_col):
        feat_row[:, t * tri:(t + 1) * tri] = features(row_cen[t], True)
    for r in range(n_row):
        feat_col[:, r * tri:(r + 1) * tri] = features(col_cen[r], False)

    step = 128

    def make_tile(t, carry):
        at = pl.ds(pl.multiple_of(t * step, step), step)
        dist = lax.dot_general(
            feat_row[:, at], feat_col[...], (((0,), (0,)), ((), ())), preferred_element_type=F32
        )
        inv = lax.rsqrt(dist)
        turns = dist * inv
        r = turns - jnp.round(turns)
        s = r * r
        tile[at, 0:n_cols] = (inv * horner(COS, s, AMP)).astype(BF16)
        tile[at, n_cols:2 * n_cols] = ((inv * r) * horner(SIN, s, -AMP)).astype(BF16)
        return carry

    n_steps = n_col * tri // step
    first = n_steps * 5 // 8
    lax.fori_loop(0, first, make_tile, 0)

    def charges_of(sweep):
        wait = remote(b_out.at[rest], b_in.at[sweep, rest], K_B + sweep, nobody)
        wait.wait_recv()
        if sweep == 0:
            labels = remote(lab_out.at[pl.ds(1, devices - 1)], lab_in.at[pl.ds(1, devices - 1)], K_LAB, nobody)
            labels.wait_send()
            labels.wait_recv()

            def gather(d, carry):
                lab_flat[pl.ds(d, 1), :] = lab_in[d]
                return carry

            lax.fori_loop(0, devices, gather, 0)
            group = chunk // slots
            widen = jnp.where(
                lax.div(iota((chunk, group), 0), slots) == iota((chunk, group), 1), 1.0, 0.0
            ).astype(BF16)
            keep = jnp.where(
                lax.rem(iota((chunk, 128), 0), slots) == iota((chunk, 128), 1), 1.0, 0.0
            )
            ones = jnp.ones((128, tri), BF16)
            target = (iota((chunk, tri), 1) + 1).astype(F32)

            def fill_pick(h, carry):
                here = lab_flat[pl.ds(pl.multiple_of(h * group, group), group), :].astype(BF16)
                wide = jnp.dot(widen, here, preferred_element_type=F32) * keep
                label = jnp.dot(wide.astype(BF16), ones, preferred_element_type=F32)
                pick[pl.ds(pl.multiple_of(h * chunk, chunk), chunk), :] = jnp.where(
                    label == target, 1.0, 0.0
                ).astype(BF16)
                return carry

            lax.fori_loop(0, cells // chunk, fill_pick, 0)
        charges = lax.dot_general(
            pick[...], b_in[sweep], (((0,), (0,)), ((), ())), preferred_element_type=F32
        ).astype(BF16)
        q_in[sweep, 0:tri, :] = charges

        def send(r, carry):
            remote(
                q_in.at[sweep, pl.ds(0, tri)],
                q_in.at[sweep, pl.ds(pl.multiple_of(r * tri, tri), tri)],
                K_Q + sweep, row_ahead(r),
            ).start()
            return carry

        lax.fori_loop(1, n_row, send, 0)
        wait.wait_send()

    for sweep in range(n_sweeps):
        charges_of(sweep)
        if sweep == 0:
            lax.fori_loop(first, n_steps, make_tile, 0)
        others = pl.ds(tri, n_cols - tri)
        q_wait = remote(q_in.at[sweep, others], q_in.at[sweep, others], K_Q + sweep, nobody)
        q_wait.wait_recv()

        def fill_qq(r, carry):
            at = pl.ds(pl.multiple_of(r * tri, tri), tri)
            below = pl.ds(pl.multiple_of(n_cols + r * tri, tri), tri)
            q = q_in[sweep, at, :]
            qq[at, :] = q
            qq[below, 0:half] = -q[:, half:]
            qq[below, half:] = q[:, :half]
            return carry

        lax.fori_loop(0, n_row, fill_qq, 0)

        def partial(t):
            at = pl.ds(pl.multiple_of(t * tri, tri), tri)
            return jnp.dot(tile[at, :], qq[...], preferred_element_type=F32)

        def one_owner(t, carry):
            rs_out[t] = partial(t).astype(BF16)
            remote(rs_out.at[t], rs_in.at[sweep, t], K_R + sweep, col_ahead(t + 1)).start()
            return carry

        lax.fori_loop(0, n_col - 1, one_owner, 0)
        total = partial(n_col - 1)
        pieces = pl.ds(0, n_col - 1)
        r_wait = remote(rs_out.at[pieces], rs_in.at[sweep, pieces], K_R + sweep, nobody)
        r_wait.wait_recv()
        q_wait.wait_send()
        for t in range(n_col - 1):
            total = total + rs_in[sweep, t].astype(F32)
        potential = total.astype(BF16)
        if sweep == n_sweeps - 1:
            pot_ref[...] = potential

        def fill_answers(h, carry):
            at = pl.ds(pl.multiple_of(h * chunk, chunk), chunk)
            f_out[at, :] = jnp.dot(pick[at, :], potential, preferred_element_type=F32).astype(BF16)
            return carry

        lax.fori_loop(0, cells // chunk, fill_answers, 0)

        def send_back(d, carry):
            remote(f_out.at[block(d)], f_in.at[sweep, block(d)], K_F + sweep, behind(d)).start()
            return carry

        lax.fori_loop(1, devices, send_back, 0)
        f_in[sweep, 0:slots, :] = f_out[0:slots, :]
        f_wait = remote(f_out.at[rest], f_in.at[sweep, rest], K_F + sweep, nobody)
        r_wait.wait_send()
        f_wait.wait_recv()
        slope = lax.dot_general(
            place[...], f_in[sweep], (((0,), (0,)), ((), ())), preferred_element_type=F32
        )
        updated = (cur[...].astype(F32) - w_ref[sweep] * slope).astype(BF16)
        if sweep == n_sweeps - 1:
            upd_ref[...] = updated
        else:
            cur[...] = updated
            fill_out()
            send_currents(sweep + 1)
            b_in[sweep + 1, 0:slots, :] = b_out[0:slots, :]
        f_wait.wait_send()


def solution(mesh):
    n_row, n_col = mesh.shape["row"], mesh.shape["col"]
    devices = n_row * n_col

    def per_device(currents, incidence, centroids, sweep_weights):
        edge_dev, width = currents.shape
        tri = centroids.shape[1]
        n_sweeps = sweep_weights.shape[0]
        slots = 16
        cells = devices * slots
        vm = pltpu.VMEM
        return pl.pallas_call(
            functools.partial(kernel, n_row, n_col),
            out_shape=(
                jax.ShapeDtypeStruct((edge_dev, width), BF16),
                jax.ShapeDtypeStruct((tri, width), BF16),
            ),
            in_specs=[pl.BlockSpec(memory_space=pltpu.VMEM)] * 3
            + [pl.BlockSpec(memory_space=pltpu.SMEM)],
            out_specs=(pl.BlockSpec(memory_space=pltpu.VMEM),) * 2,
            scratch_shapes=[
                vm((n_col * tri, 2 * n_row * tri), BF16),
                vm((cells, width), BF16),
                vm((n_sweeps, cells, width), BF16),
                vm((cells, width), BF16),
                vm((n_sweeps, cells, width), BF16),
                vm((n_sweeps, n_row * tri, width), BF16),
                vm((n_col - 1, tri, width), BF16),
                vm((n_sweeps, n_col - 1, tri, width), BF16),
                vm((2 * n_row * tri, width), BF16),
                vm((cells, edge_dev), BF16),
                vm((cells, tri), BF16),
                vm((devices, 128), F32),
                vm((devices, 1, 128), F32),
                vm((devices, 1, 128), F32),
                vm((n_col, 3, tri), jnp.int32),
                vm((n_row, 3, tri), jnp.int32),
                vm((16, n_col * tri), BF16),
                vm((16, n_row * tri), BF16),
                vm((edge_dev, width), BF16),
                pltpu.SemaphoreType.DMA((3 + 4 * n_sweeps,)),
                pltpu.SemaphoreType.DMA((3 + 4 * n_sweeps,)),
            ],
            compiler_params=pltpu.CompilerParams(
                collective_id=0, has_side_effects=True, vmem_limit_bytes=66000000
            ),
            name="sweeps",
        )(currents, incidence, centroids, sweep_weights)

    in_specs = (P(("row", "col"), None), P(None, ("row", "col")), P(None, ("row", "col")), P())
    out_specs = (P(("row", "col"), None), P(("row", "col"), None))
    return jax.shard_map(
        per_device, mesh=mesh, in_specs=in_specs, out_specs=out_specs, check_vma=False
    )
```

```python
import functools

import jax
import jax.numpy as jnp
from jax import lax
from jax.experimental import pallas as pl
from jax.experimental.pallas import tpu as pltpu
from jax.sharding import PartitionSpec as P

MESH = pl.DeviceIdType.MESH
F32 = jnp.float32
BF16 = jnp.bfloat16

AMP = 0.2 / 32.0
ROOT = (2.0 * AMP) ** 0.5
SIN = (3.14158202, -5.1671428, 2.54189902, -0.554636165)
COS = (0.999999953, -4.93479286, 4.05841191, -1.33188016, 0.219696799)


def iota(shape, dim):
    return lax.broadcasted_iota(jnp.int32, shape, dim)


def horner(coefs, s, scale):
    acc = jnp.float32(coefs[-1] * scale)
    for c in coefs[-2::-1]:
        acc = acc * s + jnp.float32(c * scale)
    return acc


def features(points, as_rows):
    n = points.shape[1]
    x, y, z = points[0:1], points[1:2], points[2:3]
    norm = x * x + y * y + z * z
    if as_rows:
        norm = norm + 1
    top = norm - (norm & 511)
    low = norm & 511
    mid = low - (low & 1)
    bit = low & 1
    one = jnp.ones((1, n), jnp.int32)
    if as_rows:
        rows = [x, y, z, top, mid, bit, one, one, one]
        scale = 1.0
    else:
        rows = [-2 * x, -2 * y, -2 * z, one, one, one, top, mid, bit]
        scale = 1.0 / 1024.0
    at = iota((16, n), 0)
    out = jnp.zeros((16, n), F32)
    for k, row in enumerate(rows):
        out = jnp.where(at == k, row.astype(F32) * scale, out)
    return out.astype(BF16)


def kernel(
    n_row, n_col,
    cur_ref, inc_ref, cen_ref, w_ref,
    upd_ref, pot_ref,
    tile_a, tile_b, b_out, b_in, f_out, f_in, q_in, qq, place, pick,
    rs_a, rs_b, own_a, own_b, p1a, p1b, rs2a, rs2b, p2a, p2b,
    lab_flat, lab_out, lab_in, row_cen, col_cen, feat_row, feat_col, cur, pot,
    send_sem, recv_sem,
):
    devices = n_row * n_col
    edge_dev, width = cur_ref.shape
    half = width // 2
    tri = cen_ref.shape[1]
    cells = b_out.shape[0]
    slots = cells // devices
    n_cols = n_row * tri
    n_sweeps = w_ref.shape[0]
    side = 4
    my_row, my_col = lax.axis_index("row"), lax.axis_index("col")
    me = my_row * n_col + my_col
    mx, mc = lax.div(my_row, 2), lax.rem(my_row, 2)
    mz, my = lax.div(my_col, side), lax.rem(my_col, side)

    def flat_id(index):
        return (lax.div(index, n_col), lax.rem(index, n_col))

    def ahead(d):
        return flat_id(lax.rem(me + d, devices))

    def behind(d):
        return flat_id(lax.rem(me + devices - d, devices))

    def along_row(dx, dc):
        return (lax.rem(mx + dx, side) * 2 + lax.rem(mc + dc, 2), my_col)

    def along_col(dz, dy):
        return (my_row, lax.rem(mz + dz, side) * side + lax.rem(my + dy, side))

    sends, recvs = [0], [0]

    def new(count, many):
        count[0] += many
        return count[0] - many

    S_ROWC, S_COLC, S_LAB = (new(sends, 1) for _ in range(3))
    R_ROWC, R_COLC, R_LAB = (new(recvs, 1) for _ in range(3))
    S_B, S_Q, S_A1, S_B1, S_A2, S_B2, S_F = (new(sends, n_sweeps) for _ in range(7))
    R_B, R_Q2, R_B1, R_A2, R_B2, R_F = (new(recvs, n_sweeps) for _ in range(6))
    R_Q1, R_A1 = (new(recvs, n_sweeps * side) for _ in range(2))

    def remote(src, dst, s, r, device):
        return pltpu.make_async_remote_copy(
            src_ref=src, dst_ref=dst, send_sem=send_sem.at[s], recv_sem=recv_sem.at[r],
            device_id=device, device_id_type=MESH,
        )

    barrier = pltpu.get_barrier_semaphore()

    def greet(d, carry):
        pl.semaphore_signal(barrier, inc=1, device_id=ahead(devices - d), device_id_type=MESH)
        return carry

    lax.fori_loop(1, devices, greet, 0)

    both = jnp.concatenate([inc_ref[0:1, :], inc_ref[1:2, :]], axis=1)
    n_con = both.shape[1]
    owner = lax.shift_right_logical(both, tri.bit_length() - 1)
    local = (both & (tri - 1)).astype(F32)
    rel = (owner - me + devices) & (devices - 1)
    hits = jnp.where(rel == iota((devices, n_con), 0), 1.0, 0.0)
    hits16 = hits.astype(BF16)
    earlier = jnp.where(iota((n_con, n_con), 0) < iota((n_con, n_con), 1), 1.0, 0.0).astype(BF16)
    before = jnp.dot(hits16, earlier, preferred_element_type=F32)
    rank = jnp.sum(hits * before, axis=0, keepdims=True)
    slot = rel.astype(F32) * float(slots) + rank
    marks = jnp.where(rank == iota((128, n_con), 0).astype(F32), local + 1.0, 0.0).astype(BF16)
    lab_flat[...] = lax.dot_general(
        hits16, marks, (((1,), (1,)), ((), ())), preferred_element_type=F32
    )
    slot_plus, slot_minus = slot[:, :edge_dev], slot[:, edge_dev:]

    def spread(d, carry):
        lab_out[d] = lab_flat[pl.ds(d, 1), :]
        return carry

    lax.fori_loop(0, devices, spread, 0)
    chunk = 256
    group = chunk // slots
    cur[...] = cur_ref[...]

    def part(h, size):
        return pl.ds(pl.multiple_of(h * size, size), size)

    def block(d):
        return part(d, slots)

    rest = pl.ds(slots, cells - slots)
    nobody = ahead(1)

    def fill_place(h, carry):
        at = (iota((chunk, edge_dev), 0) + h * chunk).astype(F32)
        rows = jnp.where(slot_plus == at, 1.0, 0.0) - jnp.where(slot_minus == at, 1.0, 0.0)
        place[part(h, chunk), :] = rows.astype(BF16)
        return carry

    lax.fori_loop(0, cells // chunk, fill_place, 0)

    def fill_out(h):
        at = part(h, chunk)
        b_out[at, :] = jnp.dot(place[at, :], cur[...], preferred_element_type=F32).astype(BF16)

    def send_out(sweep, h):
        def one(j, carry):
            d = h * group + j

            @pl.when(d > 0)
            def _():
                remote(b_out.at[block(d)], b_in.at[sweep, block(d)], S_B + sweep, R_B + sweep, ahead(d)).start()

            return carry

        lax.fori_loop(0, group, one, 0)

    def fill_first(h, carry):
        fill_out(h)
        return carry

    lax.fori_loop(0, cells // chunk, fill_first, 0)
    pl.semaphore_wait(barrier, devices - 1)

    def send_row_cen(k, carry):
        to = along_col(lax.div(k, side) + 1, lax.rem(k, side) + 1)
        remote(cen_ref, row_cen.at[k], S_ROWC, R_ROWC, to).start()
        return carry

    def send_col_cen(r, carry):
        to = along_row(lax.rem(r, side), lax.div(r, side))
        remote(cen_ref, col_cen.at[r], S_COLC, R_COLC, to).start()
        return carry

    lax.fori_loop(1, n_row, send_col_cen, 0)
    lax.fori_loop(0, n_col - 1, send_row_cen, 0)

    def send_labels(d, carry):
        remote(lab_out.at[d], lab_in.at[d], S_LAB, R_LAB, ahead(d)).start()
        return carry

    lax.fori_loop(1, devices, send_labels, 0)

    def send_first(h, carry):
        send_out(0, h)
        return carry

    lax.fori_loop(0, cells // chunk, send_first, 0)
    b_in[0, 0:slots, :] = b_out[0:slots, :]
    lab_in[0] = lab_out[0]
    row_cen[n_col - 1] = cen_ref[...]
    col_cen[0] = cen_ref[...]

    drop_rows = pl.ds(0, n_col - 1)
    drop_cols = pl.ds(1, n_row - 1)
    row_wait = remote(row_cen.at[drop_rows], row_cen.at[drop_rows], S_ROWC, R_ROWC, nobody)
    col_wait = remote(col_cen.at[drop_cols], col_cen.at[drop_cols], S_COLC, R_COLC, nobody)
    col_wait.wait_send()
    col_wait.wait_recv()
    for r in range(n_row):
        feat_col[:, r * tri:(r + 1) * tri] = features(col_cen[r], False)
    row_wait.wait_send()
    row_wait.wait_recv()
    for t in range(n_col):
        feat_row[:, t * tri:(t + 1) * tri] = features(row_cen[t], True)

    step = 128

    def make_tile(tile, k, base):
        for u in range(tri // step):
            at = pl.ds(pl.multiple_of(k * tri + u * step, step), step)
            here = pl.ds(pl.multiple_of((k - base) * tri + u * step, step), step)
            dist = lax.dot_general(
                feat_row[:, at], feat_col[...], (((0,), (0,)), ((), ())), preferred_element_type=F32
            )
            inv = lax.rsqrt(dist)
            turns = dist * inv
            r = turns - jnp.round(turns)
            s = r * r
            sine = r * horner(SIN, s, ROOT)
            cosine = horner(COS, s, -ROOT)
            tile[here, 0:n_cols] = (inv * (jnp.float32(AMP) - sine * sine)).astype(BF16)
            tile[here, n_cols:2 * n_cols] = (inv * (sine * cosine)).astype(BF16)

    def make_a(k, carry):
        make_tile(tile_a, k, 0)
        return carry

    n_a = n_col // 2
    cut1, cut2 = 5, 7
    lax.fori_loop(0, cut1, make_a, 0)

    def fill_qq(sweep, r):
        at = pl.ds(r * tri, tri)
        below = pl.ds(n_cols + r * tri, tri)
        q = q_in[sweep, at, :]
        qq[at, :] = q
        qq[below, 0:half] = -q[:, half:]
        qq[below, half:] = q[:, :half]

    def charges_of(sweep):
        wait = remote(b_out.at[rest], b_in.at[sweep, rest], S_B + sweep, R_B + sweep, nobody)
        if sweep == 0:
            labels = remote(
                lab_out.at[pl.ds(1, devices - 1)], lab_in.at[pl.ds(1, devices - 1)], S_LAB, R_LAB, nobody
            )
            labels.wait_send()
            labels.wait_recv()

            def gather(d, carry):
                lab_flat[pl.ds(d, 1), :] = lab_in[d]
                return carry

            lax.fori_loop(0, devices, gather, 0)
            widen = jnp.where(
                lax.div(iota((chunk, group), 0), slots) == iota((chunk, group), 1), 1.0, 0.0
            ).astype(BF16)
            keep = jnp.where(
                lax.rem(iota((chunk, 128), 0), slots) == iota((chunk, 128), 1), 1.0, 0.0
            )
            ones = jnp.ones((128, tri), BF16)
            target = (iota((chunk, tri), 1) + 1).astype(F32)

            def fill_pick(h, carry):
                here = lab_flat[part(h, group), :].astype(BF16)
                wide = jnp.dot(widen, here, preferred_element_type=F32) * keep
                label = jnp.dot(wide.astype(BF16), ones, preferred_element_type=F32)
                pick[part(h, chunk), :] = jnp.where(label == target, 1.0, 0.0).astype(BF16)
                return carry

            lax.fori_loop(0, cells // chunk, fill_pick, 0)
        wait.wait_recv()
        charges = lax.dot_general(
            pick[...], b_in[sweep], (((0,), (0,)), ((), ())), preferred_element_type=F32
        ).astype(BF16)
        q_in[sweep, 0:tri, :] = charges
        mine = q_in.at[sweep, pl.ds(0, tri)]
        partner = along_row(0, 1)
        for dx in (2, 1, 3):
            remote(
                mine, q_in.at[sweep, pl.ds(dx * tri, tri)],
                S_Q + sweep, R_Q1 + sweep * side + dx, along_row(dx, 0),
            ).start()
        remote(mine, q_in.at[sweep, pl.ds(side * tri, tri)], S_Q + sweep, R_Q2 + sweep, partner).start()
        fill_qq(sweep, 0)
        if sweep == 0:
            lax.fori_loop(cut1, cut2, make_a, 0)
        for dx in (1, 3, 2):
            got = q_in.at[sweep, pl.ds(dx * tri, tri)]
            remote(got, got, S_Q + sweep, R_Q1 + sweep * side + dx, partner).wait_recv()
            remote(
                got, q_in.at[sweep, pl.ds((side + dx) * tri, tri)],
                S_Q + sweep, R_Q2 + sweep, partner,
            ).start()
            fill_qq(sweep, dx)
        if sweep == 0:
            lax.fori_loop(cut2, n_a, make_a, 0)
        far = q_in.at[sweep, pl.ds(side * tri, side * tri)]
        remote(far, far, S_Q + sweep, R_Q2 + sweep, nobody).wait_recv()
        for r in range(side, 2 * side):
            fill_qq(sweep, r)
        wait.wait_send()
        sent = q_in.at[sweep, pl.ds(tri, n_cols - tri)]
        remote(sent, sent, S_Q + sweep, R_Q2 + sweep, nobody).wait_send()

    def wait_for(ref, s, r):
        return remote(ref, ref, s, r, nobody)

    last = side - 1

    def finish_a(sweep, g):
        wait_for(p1a.at[sweep, g], S_A1 + sweep, R_A1 + sweep * side + g).wait_recv()
        total = own_a[g]
        for j in range(last):
            total = total + p1a[sweep, g, j].astype(F32)
        return total

    def finish_b(sweep, g):
        total = own_b[g]
        for j in range(last):
            total = total + p1b[sweep, j, g].astype(F32)
        return total

    def emit(sweep, k, value):
        gz, gy = lax.div(k, side), lax.rem(k, side)
        left, right = value[:, :half], value[:, half:]

        @pl.when(gy < last)
        def _():
            rs_a[k] = left.astype(BF16)
            remote(
                rs_a.at[k], p1a.at[sweep, gz, gy], S_A1 + sweep, R_A1 + sweep * side + gz,
                along_col(0, last - gy),
            ).start()

        @pl.when(gz < last)
        def _():
            rs_b[k] = right.astype(BF16)
            remote(
                rs_b.at[k], p1b.at[sweep, gz, gy], S_B1 + sweep, R_B1 + sweep,
                along_col(last - gz, 0),
            ).start()

        @pl.when(gy == last)
        def _():
            own_a[gz] = left

        @pl.when(gz == last)
        def _():
            own_b[gy] = right

        @pl.when(jnp.logical_and(gy == last, gz > 0))
        def _():
            g = gz - 1
            rs2a[g] = finish_a(sweep, g).astype(BF16)
            remote(
                rs2a.at[g], p2a.at[sweep, g], S_A2 + sweep, R_A2 + sweep, along_col(last - g, 0)
            ).start()

    for sweep in range(n_sweeps):
        charges_of(sweep)

        def upper(k, carry):
            value = jnp.dot(tile_a[part(k, tri), :], qq[...], preferred_element_type=F32)
            if sweep == 0:
                make_tile(tile_b, k + n_a, n_a)
            emit(sweep, k, value)
            return carry

        def lower(k, carry):
            value = jnp.dot(tile_b[part(k - n_a, tri), :], qq[...], preferred_element_type=F32)
            emit(sweep, k, value)
            return carry

        lax.fori_loop(0, n_a, upper, 0)
        lax.fori_loop(n_a, n_col, lower, 0)
        wait_for(p1b.at[sweep], S_B1 + sweep, R_B1 + sweep).wait_recv()
        for g in range(last):
            rs2b[g] = finish_b(sweep, g).astype(BF16)
            remote(
                rs2b.at[g], p2b.at[sweep, g], S_B2 + sweep, R_B2 + sweep, along_col(0, last - g)
            ).start()
        left = finish_a(sweep, last)
        right = finish_b(sweep, last)
        wait_for(p2a.at[sweep], S_A2 + sweep, R_A2 + sweep).wait_recv()
        for j in range(last):
            left = left + p2a[sweep, j].astype(F32)
        pot[:, :half] = left.astype(BF16)
        wait_for(p2b.at[sweep], S_B2 + sweep, R_B2 + sweep).wait_recv()
        for j in range(last):
            right = right + p2b[sweep, j].astype(F32)
        pot[:, half:] = right.astype(BF16)

        def answer(h, carry):
            at = part(h, chunk)
            f_out[at, :] = jnp.dot(pick[at, :], pot[...], preferred_element_type=F32).astype(BF16)

            def send_back(j, carry):
                d = h * group + j

                @pl.when(d > 0)
                def _():
                    remote(
                        f_out.at[block(d)], f_in.at[sweep, block(d)], S_F + sweep, R_F + sweep, behind(d)
                    ).start()

                return carry

            lax.fori_loop(0, group, send_back, 0)
            return carry

        lax.fori_loop(0, cells // chunk, answer, 0)
        f_in[sweep, 0:slots, :] = f_out[0:slots, :]
        if sweep == n_sweeps - 1:
            pot_ref[...] = pot[...]
        f_wait = remote(f_out.at[rest], f_in.at[sweep, rest], S_F + sweep, R_F + sweep, nobody)
        wait_for(rs_a.at[pl.ds(0, last * side)], S_A1 + sweep, R_B1 + sweep).wait_send()
        wait_for(rs_b.at[pl.ds(0, last * side)], S_B1 + sweep, R_B1 + sweep).wait_send()
        wait_for(rs2a, S_A2 + sweep, R_A2 + sweep).wait_send()
        wait_for(rs2b, S_B2 + sweep, R_B2 + sweep).wait_send()
        f_wait.wait_recv()
        slope = lax.dot_general(
            place[...], f_in[sweep], (((0,), (0,)), ((), ())), preferred_element_type=F32
        )
        updated = (cur[...].astype(F32) - w_ref[sweep] * slope).astype(BF16)
        if sweep == n_sweeps - 1:
            upd_ref[...] = updated
        else:
            cur[...] = updated

            def next_out(h, carry):
                fill_out(h)
                send_out(sweep + 1, h)
                return carry

            lax.fori_loop(0, cells // chunk, next_out, 0)
            b_in[sweep + 1, 0:slots, :] = b_out[0:slots, :]
        f_wait.wait_send()


def solution(mesh):
    n_row, n_col = mesh.shape["row"], mesh.shape["col"]
    devices = n_row * n_col

    def per_device(currents, incidence, centroids, sweep_weights):
        edge_dev, width = currents.shape
        tri = centroids.shape[1]
        n_sweeps = sweep_weights.shape[0]
        slots = 16
        cells = devices * slots
        vm = pltpu.VMEM
        return pl.pallas_call(
            functools.partial(kernel, n_row, n_col),
            out_shape=(
                jax.ShapeDtypeStruct((edge_dev, width), BF16),
                jax.ShapeDtypeStruct((tri, width), BF16),
            ),
            in_specs=[pl.BlockSpec(memory_space=pltpu.VMEM)] * 3
            + [pl.BlockSpec(memory_space=pltpu.SMEM)],
            out_specs=(pl.BlockSpec(memory_space=pltpu.VMEM),) * 2,
            scratch_shapes=[
                vm((n_col * tri // 2, 2 * n_row * tri), BF16),
                vm((n_col * tri // 2, 2 * n_row * tri), BF16),
                vm((cells, width), BF16),
                vm((n_sweeps, cells, width), BF16),
                vm((cells, width), BF16),
                vm((n_sweeps, cells, width), BF16),
                vm((n_sweeps, n_row * tri, width), BF16),
                vm((2 * n_row * tri, width), BF16),
                vm((cells, edge_dev), BF16),
                vm((cells, tri), BF16),
                vm((n_col, tri, width // 2), BF16),
                vm((n_col, tri, width // 2), BF16),
                vm((4, tri, width // 2), F32),
                vm((4, tri, width // 2), F32),
                vm((n_sweeps, 4, 3, tri, width // 2), BF16),
                vm((n_sweeps, 3, 4, tri, width // 2), BF16),
                vm((3, tri, width // 2), BF16),
                vm((3, tri, width // 2), BF16),
                vm((n_sweeps, 3, tri, width // 2), BF16),
                vm((n_sweeps, 3, tri, width // 2), BF16),
                vm((devices, 128), F32),
                vm((devices, 1, 128), F32),
                vm((devices, 1, 128), F32),
                vm((n_col, 3, tri), jnp.int32),
                vm((n_row, 3, tri), jnp.int32),
                vm((16, n_col * tri), BF16),
                vm((16, n_row * tri), BF16),
                vm((edge_dev, width), BF16),
                vm((tri, width), BF16),
                pltpu.SemaphoreType.DMA((3 + 7 * n_sweeps,)),
                pltpu.SemaphoreType.DMA((3 + 14 * n_sweeps,)),
            ],
            compiler_params=pltpu.CompilerParams(
                collective_id=0, has_side_effects=True, vmem_limit_bytes=66000000
            ),
            name="sweeps",
        )(currents, incidence, centroids, sweep_weights)

    in_specs = (P(("row", "col"), None), P(None, ("row", "col")), P(None, ("row", "col")), P())
    out_specs = (P(("row", "col"), None), P(("row", "col"), None))
    return jax.shard_map(
        per_device, mesh=mesh, in_specs=in_specs, out_specs=out_specs, check_vma=False
    )
```

```python
import functools

import jax
import jax.numpy as jnp
from jax import lax
from jax.experimental import pallas as pl
from jax.experimental.pallas import tpu as pltpu
from jax.sharding import PartitionSpec as P

MESH = pl.DeviceIdType.MESH
F32 = jnp.float32
BF16 = jnp.bfloat16

AMP = 0.2 / 32.0
ROOT = (2.0 * AMP) ** 0.5
SIN = (3.14158202, -5.1671428, 2.54189902, -0.554636165)
COS = (0.999999953, -4.93479286, 4.05841191, -1.33188016, 0.219696799)


def iota(shape, dim):
    return lax.broadcasted_iota(jnp.int32, shape, dim)


def horner(coefs, s, scale):
    acc = jnp.float32(coefs[-1] * scale)
    for c in coefs[-2::-1]:
        acc = acc * s + jnp.float32(c * scale)
    return acc


def features(points, as_rows):
    n = points.shape[1]
    x, y, z = points[0:1], points[1:2], points[2:3]
    norm = x * x + y * y + z * z
    if as_rows:
        norm = norm + 1
    top = norm - (norm & 511)
    low = norm & 511
    mid = low - (low & 1)
    bit = low & 1
    one = jnp.ones((1, n), jnp.int32)
    if as_rows:
        rows = [x, y, z, top, mid, bit, one, one, one]
        scale = 1.0
    else:
        rows = [-2 * x, -2 * y, -2 * z, one, one, one, top, mid, bit]
        scale = 1.0 / 1024.0
    at = iota((16, n), 0)
    out = jnp.zeros((16, n), F32)
    for k, row in enumerate(rows):
        out = jnp.where(at == k, row.astype(F32) * scale, out)
    return out.astype(BF16)


def kernel(
    n_row, n_col,
    cur_ref, inc_ref, cen_ref, w_ref,
    upd_ref, pot_ref,
    tile_a, tile_b, b_out, b_in, f_out, f_in, q_in, qq, place, place_t, pick, pick_t,
    rs_a, rs_b, own_a, own_b, p1a, p1b, rs2a, rs2b, p2a, p2b,
    lab_flat, lab_out, lab_in, row_cen, col_cen, feat_row, feat_col, cur, pot,
    send_sem, recv_sem,
):
    devices = n_row * n_col
    edge_dev, width = cur_ref.shape
    half = width // 2
    tri = cen_ref.shape[1]
    cells = b_out.shape[1]
    slots = cells // devices
    n_cols = n_row * tri
    n_sweeps = w_ref.shape[0]
    side = 4
    my_row, my_col = lax.axis_index("row"), lax.axis_index("col")
    me = my_row * n_col + my_col
    mx, mc = lax.div(my_row, 2), lax.rem(my_row, 2)
    mz, my = lax.div(my_col, side), lax.rem(my_col, side)

    def flat_id(index):
        return (lax.div(index, n_col), lax.rem(index, n_col))

    def ahead(d):
        return flat_id(lax.rem(me + d, devices))

    def behind(d):
        return flat_id(lax.rem(me + devices - d, devices))

    def along_row(dx, dc):
        return (lax.rem(mx + dx, side) * 2 + lax.rem(mc + dc, 2), my_col)

    def along_col(dz, dy):
        return (my_row, lax.rem(mz + dz, side) * side + lax.rem(my + dy, side))

    sends, recvs = [0], [0]

    def new(count, many):
        count[0] += many
        return count[0] - many

    S_ROWC, S_COLC, S_LAB = (new(sends, 1) for _ in range(3))
    R_ROWC, R_COLC, R_LAB = (new(recvs, 1) for _ in range(3))
    S_A1, S_B1, S_A2, S_B2 = (new(sends, n_sweeps) for _ in range(4))
    S_B, S_Q, S_F = (new(sends, 2 * n_sweeps) for _ in range(3))
    R_B1, R_A2, R_B2 = (new(recvs, n_sweeps) for _ in range(3))
    R_B, R_Q2, R_F = (new(recvs, 2 * n_sweeps) for _ in range(3))
    R_A1 = new(recvs, n_sweeps * side)
    R_Q1 = new(recvs, 2 * n_sweeps * side)

    def remote(src, dst, s, r, device):
        return pltpu.make_async_remote_copy(
            src_ref=src, dst_ref=dst, send_sem=send_sem.at[s], recv_sem=recv_sem.at[r],
            device_id=device, device_id_type=MESH,
        )

    barrier = pltpu.get_barrier_semaphore()

    def greet(h, carry):
        for j in range(8):
            d = devices - 1 - h * 8 - j
            pl.semaphore_signal(barrier, inc=1, device_id=ahead(d), device_id_type=MESH)
        return carry

    lax.fori_loop(0, devices // 8 - 1, greet, 0)
    for d in range(1, 8):
        pl.semaphore_signal(barrier, inc=1, device_id=ahead(d), device_id_type=MESH)

    both = jnp.concatenate([inc_ref[0:1, :], inc_ref[1:2, :]], axis=1)
    n_con = both.shape[1]
    owner = lax.shift_right_logical(both, tri.bit_length() - 1)
    local = (both & (tri - 1)).astype(F32)
    rel = (owner - me + devices) & (devices - 1)
    hits = jnp.where(rel == iota((devices, n_con), 0), 1.0, 0.0)
    hits16 = hits.astype(BF16)
    earlier = jnp.where(iota((n_con, n_con), 0) < iota((n_con, n_con), 1), 1.0, 0.0).astype(BF16)
    before = jnp.dot(hits16, earlier, preferred_element_type=F32)
    rank = jnp.sum(hits * before, axis=0, keepdims=True)
    slot = rel.astype(F32) * float(slots) + rank
    marks = jnp.where(rank == iota((128, n_con), 0).astype(F32), local + 1.0, 0.0).astype(BF16)
    lab_flat[...] = lax.dot_general(
        hits16, marks, (((1,), (1,)), ((), ())), preferred_element_type=F32
    )
    slot_plus, slot_minus = slot[:, :edge_dev], slot[:, edge_dev:]

    def spread(d, carry):
        lab_out[d] = lab_flat[pl.ds(d, 1), :]
        return carry

    lax.fori_loop(0, devices, spread, 0)
    chunk = 256
    group = chunk // slots
    for c in range(2):
        cur[c] = cur_ref[:, c * half:(c + 1) * half]

    def part(h, size):
        return pl.ds(h * size if isinstance(h, int) else pl.multiple_of(h * size, size), size)

    def block(d):
        return part(d, slots)

    rest = pl.ds(slots, cells - slots)
    nobody = ahead(1)

    def fill_place(h, carry):
        at = (iota((chunk, edge_dev), 0) + h * chunk).astype(F32)
        rows = jnp.where(slot_plus == at, 1.0, 0.0) - jnp.where(slot_minus == at, 1.0, 0.0)
        place[part(h, chunk), :] = rows.astype(BF16)
        place_t[:, part(h, chunk)] = rows.T.astype(BF16)
        return carry

    lax.fori_loop(0, cells // chunk, fill_place, 0)

    def fill_out(c, h):
        at = part(h, chunk)
        b_out[c, at, :] = jnp.dot(place[at, :], cur[c], preferred_element_type=F32).astype(BF16)

    def first_of(h):
        return range(1 if isinstance(h, int) else 0, group)

    def send_out(sweep, c, h):
        for j in first_of(h):
            d = h * group + j
            remote(
                b_out.at[c, block(d)], b_in.at[sweep, c, block(d)],
                S_B + 2 * sweep + c, R_B + 2 * sweep + c, ahead(d),
            ).start()

    def all_chunks(one):
        one(0)

        def other(h, carry):
            one(h)
            return carry

        lax.fori_loop(1, cells // chunk, other, 0)

    def fill_first(h, carry):
        fill_out(0, h)
        fill_out(1, h)
        return carry

    lax.fori_loop(0, cells // chunk, fill_first, 0)
    pl.semaphore_wait(barrier, devices - 1)

    def send_row_cen(k, carry):
        to = along_col(lax.div(k, side) + 1, lax.rem(k, side) + 1)
        remote(cen_ref, row_cen.at[k], S_ROWC, R_ROWC, to).start()
        return carry

    def send_col_cen(r, carry):
        to = along_row(lax.rem(r, side), lax.div(r, side))
        remote(cen_ref, col_cen.at[r], S_COLC, R_COLC, to).start()
        return carry

    lax.fori_loop(1, n_row, send_col_cen, 0)
    lax.fori_loop(0, n_col - 1, send_row_cen, 0)

    def send_labels(h):
        for j in first_of(h):
            d = h * group + j
            remote(lab_out.at[d], lab_in.at[d], S_LAB, R_LAB, ahead(d)).start()

    def send_first(h):
        for j in first_of(h):
            d = h * group + j
            remote(b_out.at[:, block(d)], b_in.at[0, :, block(d)], S_B, R_B, ahead(d)).start()

    all_chunks(send_labels)
    all_chunks(send_first)
    b_in[0, :, 0:slots, :] = b_out[:, 0:slots, :]
    lab_in[0] = lab_out[0]
    row_cen[n_col - 1] = cen_ref[...]
    col_cen[0] = cen_ref[...]

    drop_rows = pl.ds(0, n_col - 1)
    drop_cols = pl.ds(1, n_row - 1)
    row_wait = remote(row_cen.at[drop_rows], row_cen.at[drop_rows], S_ROWC, R_ROWC, nobody)
    col_wait = remote(col_cen.at[drop_cols], col_cen.at[drop_cols], S_COLC, R_COLC, nobody)
    col_wait.wait_send()
    col_wait.wait_recv()
    for r in range(n_row):
        feat_col[:, r * tri:(r + 1) * tri] = features(col_cen[r], False)
    row_wait.wait_send()
    row_wait.wait_recv()
    for t in range(n_col):
        feat_row[:, t * tri:(t + 1) * tri] = features(row_cen[t], True)

    step = 128

    def make_tile(tile, k, base):
        for u in range(tri // step):
            at, here = part(k * (tri // step) + u, step), part((k - base) * (tri // step) + u, step)
            dist = lax.dot_general(
                feat_row[:, at], feat_col[...], (((0,), (0,)), ((), ())), preferred_element_type=F32
            )
            inv = lax.rsqrt(dist)
            turns = dist * inv
            r = turns - jnp.round(turns)
            s = r * r
            sine = r * horner(SIN, s, ROOT)
            cosine = horner(COS, s, -ROOT)
            tile[here, 0:n_cols] = (inv * (jnp.float32(AMP) - sine * sine)).astype(BF16)
            tile[here, n_cols:2 * n_cols] = (inv * (sine * cosine)).astype(BF16)

    def make_a(k, carry):
        make_tile(tile_a, k, 0)
        return carry

    n_a = n_col // 2
    cuts = (0, 4, 5, 6, 7, n_a)

    def more_tile(stage):
        lax.fori_loop(cuts[stage], cuts[stage + 1], make_a, 0)

    def fill_qq(sweep, c, r):
        at = pl.ds(r * tri, tri)
        below = pl.ds(n_cols + r * tri, tri)
        q = q_in[sweep, c, at, :]
        if c == 0:
            qq[at, :half] = q
            qq[below, half:] = q
        else:
            qq[at, half:] = q
            qq[below, :half] = -q

    def read_labels():
        labels = remote(
            lab_out.at[pl.ds(1, devices - 1)], lab_in.at[pl.ds(1, devices - 1)], S_LAB, R_LAB, nobody
        )
        labels.wait_send()
        labels.wait_recv()

        def gather(d, carry):
            lab_flat[pl.ds(d, 1), :] = lab_in[d]
            return carry

        lax.fori_loop(0, devices, gather, 0)
        widen = jnp.where(
            lax.div(iota((chunk, group), 0), slots) == iota((chunk, group), 1), 1.0, 0.0
        ).astype(BF16)
        keep = jnp.where(
            lax.rem(iota((chunk, 128), 0), slots) == iota((chunk, 128), 1), 1.0, 0.0
        )
        ones = jnp.ones((128, tri), BF16)
        target = (iota((chunk, tri), 1) + 1).astype(F32)

        def fill_pick(h, carry):
            here = lab_flat[part(h, group), :].astype(BF16)
            wide = jnp.dot(widen, here, preferred_element_type=F32) * keep
            label = jnp.dot(wide.astype(BF16), ones, preferred_element_type=F32)
            rows = jnp.where(label == target, 1.0, 0.0)
            pick[part(h, chunk), :] = rows.astype(BF16)
            pick_t[:, part(h, chunk)] = rows.T.astype(BF16)
            return carry

        lax.fori_loop(0, cells // chunk, fill_pick, 0)

    def charges_of(sweep):
        partner = along_row(0, 1)
        waits = []
        if sweep == 0:
            more_tile(0)
            read_labels()
        for c in range(2):
            at = 2 * sweep + c
            if sweep > 0:
                wait = remote(b_out.at[c, rest], b_in.at[sweep, c, rest], S_B + at, R_B + at, nobody)
                wait.wait_recv()
                waits.append(wait)
            elif c == 0:
                wait = remote(b_out.at[:, rest], b_in.at[0, :, rest], S_B, R_B, nobody)
                wait.wait_recv()
                waits.append(wait)
            q_in[sweep, c, 0:tri, :] = jnp.dot(
                pick_t[...], b_in[sweep, c], preferred_element_type=F32
            ).astype(BF16)
            mine = q_in.at[sweep, c, pl.ds(0, tri)]
            for dx in (2, 1, 3):
                remote(
                    mine, q_in.at[sweep, c, pl.ds(dx * tri, tri)],
                    S_Q + at, R_Q1 + at * side + dx, along_row(dx, 0),
                ).start()
            remote(mine, q_in.at[sweep, c, pl.ds(side * tri, tri)], S_Q + at, R_Q2 + at, partner).start()
            fill_qq(sweep, c, 0)
            if sweep == 0 and c == 1:
                more_tile(1)
                more_tile(2)
        for c in range(2):
            at = 2 * sweep + c
            for dx in (1, 3, 2):
                got = q_in.at[sweep, c, pl.ds(dx * tri, tri)]
                remote(got, got, S_Q + at, R_Q1 + at * side + dx, partner).wait_recv()
                remote(
                    got, q_in.at[sweep, c, pl.ds((side + dx) * tri, tri)], S_Q + at, R_Q2 + at, partner
                ).start()
                fill_qq(sweep, c, dx)
            if sweep == 0:
                more_tile(3 + c)
        for c in range(2):
            at = 2 * sweep + c
            far = q_in.at[sweep, c, pl.ds(side * tri, side * tri)]
            remote(far, far, S_Q + at, R_Q2 + at, nobody).wait_recv()
            for r in range(side, 2 * side):
                fill_qq(sweep, c, r)
            if c < len(waits):
                waits[c].wait_send()
            sent = q_in.at[sweep, c, pl.ds(tri, n_cols - tri)]
            remote(sent, sent, S_Q + at, R_Q2 + at, nobody).wait_send()

    def wait_for(ref, s, r):
        return remote(ref, ref, s, r, nobody)

    last = side - 1

    def finish_a(sweep, g):
        wait_for(p1a.at[sweep, g], S_A1 + sweep, R_A1 + sweep * side + g).wait_recv()
        total = own_a[g]
        for j in range(last):
            total = total + p1a[sweep, g, j].astype(F32)
        return total

    def finish_b(sweep, g):
        total = own_b[g]
        for j in range(last):
            total = total + p1b[sweep, j, g].astype(F32)
        return total

    def emit(sweep, k, value):
        k = jnp.int32(k)
        gz, gy = lax.div(k, side), lax.rem(k, side)
        left, right = value[:, :half], value[:, half:]

        @pl.when(gy < last)
        def _():
            rs_a[k] = left.astype(BF16)
            remote(
                rs_a.at[k], p1a.at[sweep, gz, gy], S_A1 + sweep, R_A1 + sweep * side + gz,
                along_col(0, last - gy),
            ).start()

        @pl.when(gz < last)
        def _():
            rs_b[k] = right.astype(BF16)
            remote(
                rs_b.at[k], p1b.at[sweep, gz, gy], S_B1 + sweep, R_B1 + sweep,
                along_col(last - gz, 0),
            ).start()

        @pl.when(gy == last)
        def _():
            own_a[gz] = left

        @pl.when(gz == last)
        def _():
            own_b[gy] = right

        @pl.when(jnp.logical_and(gy == last - 1, gz > 0))
        def _():
            g = gz - 1
            rs2a[g] = finish_a(sweep, g).astype(BF16)
            remote(
                rs2a.at[g], p2a.at[sweep, g], S_A2 + sweep, R_A2 + sweep, along_col(last - g, 0)
            ).start()

    for sweep in range(n_sweeps):
        charges_of(sweep)

        def close_b():
            wait_for(p1b.at[sweep], S_B1 + sweep, R_B1 + sweep).wait_recv()
            for g in range(last):
                rs2b[g] = finish_b(sweep, g).astype(BF16)
                remote(
                    rs2b.at[g], p2b.at[sweep, g], S_B2 + sweep, R_B2 + sweep, along_col(0, last - g)
                ).start()

        def upper(k, carry):
            value = jnp.dot(tile_a[part(k, tri), :], qq[...], preferred_element_type=F32)
            emit(sweep, k, value)
            return carry

        def lower(k, carry, more):
            value = jnp.dot(tile_b[part(k - n_a, tri), :], qq[...], preferred_element_type=F32)
            if more:
                make_tile(tile_b, k + 1, n_a)
            emit(sweep, k, value)
            return carry

        if sweep == 0:
            lax.fori_loop(0, n_a, upper, 0)
            make_tile(tile_b, n_a, n_a)
            lax.fori_loop(n_a, n_col - 1, functools.partial(lower, more=True), 0)
            close_b()
            lower(n_col - 1, 0, False)
        else:
            lax.fori_loop(0, n_a, upper, 0)
            lax.fori_loop(n_a, n_col, functools.partial(lower, more=False), 0)
            close_b()

        def answer(c):
            def one(h):
                at = part(h, chunk)
                f_out[c, at, :] = jnp.dot(pick[at, :], pot[c], preferred_element_type=F32).astype(BF16)
                for j in first_of(h):
                    d = h * group + j
                    remote(
                        f_out.at[c, block(d)], f_in.at[sweep, c, block(d)],
                        S_F + 2 * sweep + c, R_F + 2 * sweep + c, behind(d),
                    ).start()

            all_chunks(one)
            f_in[sweep, c, 0:slots, :] = f_out[c, 0:slots, :]
            if sweep == n_sweeps - 1:
                pot_ref[:, c * half:(c + 1) * half] = pot[c]

        left = finish_a(sweep, last)
        wait_for(p2a.at[sweep], S_A2 + sweep, R_A2 + sweep).wait_recv()
        for j in range(last):
            left = left + p2a[sweep, j].astype(F32)
        pot[0] = left.astype(BF16)
        answer(0)
        right = finish_b(sweep, last)
        wait_for(p2b.at[sweep], S_B2 + sweep, R_B2 + sweep).wait_recv()
        for j in range(last):
            right = right + p2b[sweep, j].astype(F32)
        pot[1] = right.astype(BF16)
        answer(1)
        wait_for(rs_a.at[pl.ds(0, last * side)], S_A1 + sweep, R_B1 + sweep).wait_send()
        wait_for(rs_b.at[pl.ds(0, last * side)], S_B1 + sweep, R_B1 + sweep).wait_send()
        wait_for(rs2a, S_A2 + sweep, R_A2 + sweep).wait_send()
        wait_for(rs2b, S_B2 + sweep, R_B2 + sweep).wait_send()
        for c in range(2):
            at = 2 * sweep + c
            f_wait = remote(f_out.at[c, rest], f_in.at[sweep, c, rest], S_F + at, R_F + at, nobody)
            f_wait.wait_recv()
            slope = jnp.dot(place_t[...], f_in[sweep, c], preferred_element_type=F32)
            updated = (cur[c].astype(F32) - w_ref[sweep] * slope).astype(BF16)
            if sweep == n_sweeps - 1:
                upd_ref[:, c * half:(c + 1) * half] = updated
            else:
                cur[c] = updated

                def next_out(h):
                    fill_out(c, h)
                    send_out(sweep + 1, c, h)

                all_chunks(next_out)
                b_in[sweep + 1, c, 0:slots, :] = b_out[c, 0:slots, :]
            f_wait.wait_send()


def solution(mesh):
    n_row, n_col = mesh.shape["row"], mesh.shape["col"]
    devices = n_row * n_col

    def per_device(currents, incidence, centroids, sweep_weights):
        edge_dev, width = currents.shape
        tri = centroids.shape[1]
        n_sweeps = sweep_weights.shape[0]
        slots = 16
        cells = devices * slots
        vm = pltpu.VMEM
        return pl.pallas_call(
            functools.partial(kernel, n_row, n_col),
            out_shape=(
                jax.ShapeDtypeStruct((edge_dev, width), BF16),
                jax.ShapeDtypeStruct((tri, width), BF16),
            ),
            in_specs=[pl.BlockSpec(memory_space=pltpu.VMEM)] * 3
            + [pl.BlockSpec(memory_space=pltpu.SMEM)],
            out_specs=(pl.BlockSpec(memory_space=pltpu.VMEM),) * 2,
            scratch_shapes=[
                vm((n_col * tri // 2, 2 * n_row * tri), BF16),
                vm((n_col * tri // 2, 2 * n_row * tri), BF16),
                vm((2, cells, width // 2), BF16),
                vm((n_sweeps, 2, cells, width // 2), BF16),
                vm((2, cells, width // 2), BF16),
                vm((n_sweeps, 2, cells, width // 2), BF16),
                vm((n_sweeps, 2, n_row * tri, width // 2), BF16),
                vm((2 * n_row * tri, width), BF16),
                vm((cells, edge_dev), BF16),
                vm((edge_dev, cells), BF16),
                vm((cells, tri), BF16),
                vm((tri, cells), BF16),
                vm((n_col, tri, width // 2), BF16),
                vm((n_col, tri, width // 2), BF16),
                vm((4, tri, width // 2), F32),
                vm((4, tri, width // 2), F32),
                vm((n_sweeps, 4, 3, tri, width // 2), BF16),
                vm((n_sweeps, 3, 4, tri, width // 2), BF16),
                vm((3, tri, width // 2), BF16),
                vm((3, tri, width // 2), BF16),
                vm((n_sweeps, 3, tri, width // 2), BF16),
                vm((n_sweeps, 3, tri, width // 2), BF16),
                vm((devices, 128), F32),
                vm((devices, 1, 128), F32),
                vm((devices, 1, 128), F32),
                vm((n_col, 3, tri), jnp.int32),
                vm((n_row, 3, tri), jnp.int32),
                vm((16, n_col * tri), BF16),
                vm((16, n_row * tri), BF16),
                vm((2, edge_dev, width // 2), BF16),
                vm((2, tri, width // 2), BF16),
                pltpu.SemaphoreType.DMA((3 + 10 * n_sweeps,)),
                pltpu.SemaphoreType.DMA((3 + 21 * n_sweeps,)),
            ],
            compiler_params=pltpu.CompilerParams(
                collective_id=0, has_side_effects=True, vmem_limit_bytes=66000000
            ),
            name="sweeps",
        )(currents, incidence, centroids, sweep_weights)

    in_specs = (P(("row", "col"), None), P(None, ("row", "col")), P(None, ("row", "col")), P())
    out_specs = (P(("row", "col"), None), P(("row", "col"), None))
    return jax.shard_map(
        per_device, mesh=mesh, in_specs=in_specs, out_specs=out_specs, check_vma=False
    )
```

```python
import functools

import jax
import jax.numpy as jnp
from jax import lax
from jax.experimental import pallas as pl
from jax.experimental.pallas import tpu as pltpu
from jax.sharding import PartitionSpec as P

MESH = pl.DeviceIdType.MESH
F32 = jnp.float32
BF16 = jnp.bfloat16

AMP = 0.2 / 32.0
ROOT = (2.0 * AMP) ** 0.5
SIN = (3.14158202, -5.1671428, 2.54189902, -0.554636165)
COS = (-0.11181640625, 0.55078125, -0.4453125, 0.1328125)


def iota(shape, dim):
    return lax.broadcasted_iota(jnp.int32, shape, dim)


def horner(coefs, s, scale):
    acc = jnp.float32(coefs[-1] * scale)
    for c in coefs[-2::-1]:
        acc = acc * s + jnp.float32(c * scale)
    return acc


def horner16(coefs, s):
    acc = BF16(coefs[-1])
    for c in coefs[-2::-1]:
        acc = acc * s + BF16(c)
    return acc


def features(points, as_rows):
    n = points.shape[1]
    x, y, z = points[0:1], points[1:2], points[2:3]
    norm = x * x + y * y + z * z
    if as_rows:
        norm = norm + 1
    top = norm - (norm & 511)
    low = norm & 511
    mid = low - (low & 1)
    bit = low & 1
    one = jnp.ones((1, n), jnp.int32)
    if as_rows:
        rows = [x, y, z, top, mid, bit, one, one, one]
        scale = 1.0
    else:
        rows = [-2 * x, -2 * y, -2 * z, one, one, one, top, mid, bit]
        scale = 1.0 / 1024.0
    at = iota((16, n), 0)
    out = jnp.zeros((16, n), F32)
    for k, row in enumerate(rows):
        out = jnp.where(at == k, row.astype(F32) * scale, out)
    return out.astype(BF16)


def kernel(
    n_row, n_col,
    cur_ref, inc_ref, cen_ref, w_ref,
    upd_ref, pot_ref,
    tile_a, tile_b, b_out, b_in, f_out, f_in, q_in, qq, place, place_t, pick, pick_t,
    rs_a, rs_b, own_a, own_b, p1a, p1b, rs2a, rs2b, p2a, p2b,
    lab_flat, lab_out, lab_in, row_cen, col_cen, feat_row, feat_col, cur, pot,
    send_sem, recv_sem,
):
    devices = n_row * n_col
    edge_dev, width = cur_ref.shape
    half = width // 2
    tri = cen_ref.shape[1]
    cells = b_out.shape[1]
    slots = cells // devices
    n_cols = n_row * tri
    n_sweeps = w_ref.shape[0]
    side = 4
    my_row, my_col = lax.axis_index("row"), lax.axis_index("col")
    me = my_row * n_col + my_col
    mx, mc = lax.div(my_row, 2), lax.rem(my_row, 2)
    mz, my = lax.div(my_col, side), lax.rem(my_col, side)

    def flat_id(index):
        return (lax.div(index, n_col), lax.rem(index, n_col))

    def ahead(d):
        return flat_id(lax.rem(me + d, devices))

    def behind(d):
        return flat_id(lax.rem(me + devices - d, devices))

    def along_row(dx, dc):
        return (lax.rem(mx + dx, side) * 2 + lax.rem(mc + dc, 2), my_col)

    def along_col(dz, dy):
        return (my_row, lax.rem(mz + dz, side) * side + lax.rem(my + dy, side))

    sends, recvs = [0], [0]

    def new(count, many):
        count[0] += many
        return count[0] - many

    S_ROWC, S_COLC, S_LAB = (new(sends, 1) for _ in range(3))
    R_ROWC, R_COLC, R_LAB = (new(recvs, 1) for _ in range(3))
    S_A1, S_B1, S_A2, S_B2 = (new(sends, n_sweeps) for _ in range(4))
    S_B, S_Q, S_F = (new(sends, 2 * n_sweeps) for _ in range(3))
    R_B1, R_A2, R_B2 = (new(recvs, n_sweeps) for _ in range(3))
    R_B, R_Q2, R_F = (new(recvs, 2 * n_sweeps) for _ in range(3))
    R_A1 = new(recvs, n_sweeps * side)
    R_Q1 = new(recvs, 2 * n_sweeps * side)

    def remote(src, dst, s, r, device):
        return pltpu.make_async_remote_copy(
            src_ref=src, dst_ref=dst, send_sem=send_sem.at[s], recv_sem=recv_sem.at[r],
            device_id=device, device_id_type=MESH,
        )

    barrier = pltpu.get_barrier_semaphore()

    def greet(h, carry):
        for j in range(8):
            d = devices - 1 - h * 8 - j
            pl.semaphore_signal(barrier, inc=1, device_id=ahead(d), device_id_type=MESH)
        return carry

    lax.fori_loop(0, devices // 8 - 1, greet, 0)
    for d in range(1, 8):
        pl.semaphore_signal(barrier, inc=1, device_id=ahead(d), device_id_type=MESH)

    both = jnp.concatenate([inc_ref[0:1, :], inc_ref[1:2, :]], axis=1)
    n_con = both.shape[1]
    owner = lax.shift_right_logical(both, tri.bit_length() - 1)
    local = (both & (tri - 1)).astype(F32)
    rel = (owner - me + devices) & (devices - 1)
    hits = jnp.where(rel == iota((devices, n_con), 0), 1.0, 0.0)
    hits16 = hits.astype(BF16)
    earlier = jnp.where(iota((n_con, n_con), 0) < iota((n_con, n_con), 1), 1.0, 0.0).astype(BF16)
    before = jnp.dot(hits16, earlier, preferred_element_type=F32)
    rank = jnp.sum(hits * before, axis=0, keepdims=True)
    slot = rel.astype(F32) * float(slots) + rank
    marks = jnp.where(rank == iota((128, n_con), 0).astype(F32), local + 1.0, 0.0).astype(BF16)
    lab_flat[...] = lax.dot_general(
        hits16, marks, (((1,), (1,)), ((), ())), preferred_element_type=F32
    )
    slot_plus, slot_minus = slot[:, :edge_dev], slot[:, edge_dev:]

    def spread(d, carry):
        lab_out[d] = lab_flat[pl.ds(d, 1), :]
        return carry

    lax.fori_loop(0, devices, spread, 0)
    chunk = 256
    group = chunk // slots
    for c in range(2):
        cur[c] = cur_ref[:, c * half:(c + 1) * half]

    def part(h, size):
        return pl.ds(h * size if isinstance(h, int) else pl.multiple_of(h * size, size), size)

    def block(d):
        return part(d, slots)

    rest = pl.ds(slots, cells - slots)
    nobody = ahead(1)

    def fill_place(h, carry):
        at = (iota((chunk, edge_dev), 0) + h * chunk).astype(F32)
        rows = jnp.where(slot_plus == at, 1.0, 0.0) - jnp.where(slot_minus == at, 1.0, 0.0)
        place[part(h, chunk), :] = rows.astype(BF16)
        place_t[:, part(h, chunk)] = rows.T.astype(BF16)
        return carry

    lax.fori_loop(0, cells // chunk, fill_place, 0)

    def fill_out(c, h):
        at = part(h, chunk)
        b_out[c, at, :] = jnp.dot(place[at, :], cur[c], preferred_element_type=F32).astype(BF16)

    def first_of(h):
        return range(1 if isinstance(h, int) else 0, group)

    def send_out(sweep, c, h):
        for j in first_of(h):
            d = h * group + j
            remote(
                b_out.at[c, block(d)], b_in.at[sweep, c, block(d)],
                S_B + 2 * sweep + c, R_B + 2 * sweep + c, ahead(d),
            ).start()

    def all_chunks(one):
        one(0)

        def other(h, carry):
            one(h)
            return carry

        lax.fori_loop(1, cells // chunk, other, 0)

    def fill_first(h, carry):
        fill_out(0, h)
        fill_out(1, h)
        return carry

    lax.fori_loop(0, cells // chunk, fill_first, 0)
    pl.semaphore_wait(barrier, devices - 1)

    def send_row_cen(k, carry):
        to = along_col(lax.div(k, side) + 1, lax.rem(k, side) + 1)
        remote(cen_ref, row_cen.at[k], S_ROWC, R_ROWC, to).start()
        return carry

    def send_col_cen(r, carry):
        to = along_row(lax.rem(r, side), lax.div(r, side))
        remote(cen_ref, col_cen.at[r], S_COLC, R_COLC, to).start()
        return carry

    lax.fori_loop(1, n_row, send_col_cen, 0)
    lax.fori_loop(0, n_col - 1, send_row_cen, 0)

    def send_labels(h):
        for j in first_of(h):
            d = h * group + j
            remote(lab_out.at[d], lab_in.at[d], S_LAB, R_LAB, ahead(d)).start()

    def send_first(h):
        for j in first_of(h):
            d = h * group + j
            remote(b_out.at[:, block(d)], b_in.at[0, :, block(d)], S_B, R_B, ahead(d)).start()

    all_chunks(send_labels)
    all_chunks(send_first)
    b_in[0, :, 0:slots, :] = b_out[:, 0:slots, :]
    lab_in[0] = lab_out[0]
    row_cen[n_col - 1] = cen_ref[...]
    col_cen[0] = cen_ref[...]

    drop_rows = pl.ds(0, n_col - 1)
    drop_cols = pl.ds(1, n_row - 1)
    row_wait = remote(row_cen.at[drop_rows], row_cen.at[drop_rows], S_ROWC, R_ROWC, nobody)
    col_wait = remote(col_cen.at[drop_cols], col_cen.at[drop_cols], S_COLC, R_COLC, nobody)
    col_wait.wait_send()
    col_wait.wait_recv()
    for r in range(n_row):
        feat_col[:, r * tri:(r + 1) * tri] = features(col_cen[r], False)
    row_wait.wait_send()
    row_wait.wait_recv()
    for t in range(n_col):
        feat_row[:, t * tri:(t + 1) * tri] = features(row_cen[t], True)

    step = 128

    def make_tile(tile, k, base):
        for u in range(tri // step):
            at, here = part(k * (tri // step) + u, step), part((k - base) * (tri // step) + u, step)
            dist = lax.dot_general(
                feat_row[:, at], feat_col[...], (((0,), (0,)), ((), ())), preferred_element_type=F32
            )
            inv = lax.rsqrt(dist)
            turns = dist * inv
            r = turns - jnp.round(turns)
            s = r * r
            sine = r * horner(SIN, s, ROOT)
            cosine = horner16(COS, s.astype(BF16))
            tile[here, 0:n_cols] = (inv * (jnp.float32(AMP) - sine * sine)).astype(BF16)
            tile[here, n_cols:2 * n_cols] = (inv * sine).astype(BF16) * cosine

    def make_a(k, carry):
        make_tile(tile_a, k, 0)
        return carry

    n_a = n_col // 2
    cuts = (0, 4, 5, 6, 7, n_a)

    def more_tile(stage):
        lax.fori_loop(cuts[stage], cuts[stage + 1], make_a, 0)

    def fill_qq(sweep, c, r):
        at = pl.ds(r * tri, tri)
        below = pl.ds(n_cols + r * tri, tri)
        q = q_in[sweep, c, at, :]
        if c == 0:
            qq[at, :half] = q
            qq[below, half:] = q
        else:
            qq[at, half:] = q
            qq[below, :half] = -q

    def read_labels():
        labels = remote(
            lab_out.at[pl.ds(1, devices - 1)], lab_in.at[pl.ds(1, devices - 1)], S_LAB, R_LAB, nobody
        )
        labels.wait_send()
        labels.wait_recv()

        def gather(d, carry):
            lab_flat[pl.ds(d, 1), :] = lab_in[d]
            return carry

        lax.fori_loop(0, devices, gather, 0)
        widen = jnp.where(
            lax.div(iota((chunk, group), 0), slots) == iota((chunk, group), 1), 1.0, 0.0
        ).astype(BF16)
        keep = jnp.where(
            lax.rem(iota((chunk, 128), 0), slots) == iota((chunk, 128), 1), 1.0, 0.0
        )
        ones = jnp.ones((128, tri), BF16)
        target = (iota((chunk, tri), 1) + 1).astype(F32)

        def fill_pick(h, carry):
            here = lab_flat[part(h, group), :].astype(BF16)
            wide = jnp.dot(widen, here, preferred_element_type=F32) * keep
            label = jnp.dot(wide.astype(BF16), ones, preferred_element_type=F32)
            rows = jnp.where(label == target, 1.0, 0.0)
            pick[part(h, chunk), :] = rows.astype(BF16)
            pick_t[:, part(h, chunk)] = rows.T.astype(BF16)
            return carry

        lax.fori_loop(0, cells // chunk, fill_pick, 0)

    def charges_of(sweep):
        partner = along_row(0, 1)
        waits = []
        if sweep == 0:
            more_tile(0)
            read_labels()
        for c in range(2):
            at = 2 * sweep + c
            if sweep > 0:
                wait = remote(b_out.at[c, rest], b_in.at[sweep, c, rest], S_B + at, R_B + at, nobody)
                wait.wait_recv()
                waits.append(wait)
            elif c == 0:
                wait = remote(b_out.at[:, rest], b_in.at[0, :, rest], S_B, R_B, nobody)
                wait.wait_recv()
                waits.append(wait)
            q_in[sweep, c, 0:tri, :] = jnp.dot(
                pick_t[...], b_in[sweep, c], preferred_element_type=F32
            ).astype(BF16)
            mine = q_in.at[sweep, c, pl.ds(0, tri)]
            for dx in (2, 1, 3):
                remote(
                    mine, q_in.at[sweep, c, pl.ds(dx * tri, tri)],
                    S_Q + at, R_Q1 + at * side + dx, along_row(dx, 0),
                ).start()
            remote(mine, q_in.at[sweep, c, pl.ds(side * tri, tri)], S_Q + at, R_Q2 + at, partner).start()
            fill_qq(sweep, c, 0)
            if sweep == 0 and c == 1:
                more_tile(1)
                more_tile(2)
        for c in range(2):
            at = 2 * sweep + c
            for dx in (1, 3, 2):
                got = q_in.at[sweep, c, pl.ds(dx * tri, tri)]
                remote(got, got, S_Q + at, R_Q1 + at * side + dx, partner).wait_recv()
                remote(
                    got, q_in.at[sweep, c, pl.ds((side + dx) * tri, tri)], S_Q + at, R_Q2 + at, partner
                ).start()
                fill_qq(sweep, c, dx)
            if sweep == 0:
                more_tile(3 + c)
        for c in range(2):
            at = 2 * sweep + c
            far = q_in.at[sweep, c, pl.ds(side * tri, side * tri)]
            remote(far, far, S_Q + at, R_Q2 + at, nobody).wait_recv()
            for r in range(side, 2 * side):
                fill_qq(sweep, c, r)
            if c < len(waits):
                waits[c].wait_send()
            sent = q_in.at[sweep, c, pl.ds(tri, n_cols - tri)]
            remote(sent, sent, S_Q + at, R_Q2 + at, nobody).wait_send()

    def wait_for(ref, s, r):
        return remote(ref, ref, s, r, nobody)

    last = side - 1

    def finish_a(sweep, g):
        wait_for(p1a.at[sweep, g], S_A1 + sweep, R_A1 + sweep * side + g).wait_recv()
        total = own_a[g]
        for j in range(last):
            total = total + p1a[sweep, g, j].astype(F32)
        return total

    def finish_b(sweep, g):
        total = own_b[g]
        for j in range(last):
            total = total + p1b[sweep, j, g].astype(F32)
        return total

    def emit(sweep, k, value):
        k = jnp.int32(k)
        gz, gy = lax.div(k, side), lax.rem(k, side)
        left, right = value[:, :half], value[:, half:]

        @pl.when(gy < last)
        def _():
            rs_a[k] = left.astype(BF16)
            remote(
                rs_a.at[k], p1a.at[sweep, gz, gy], S_A1 + sweep, R_A1 + sweep * side + gz,
                along_col(0, last - gy),
            ).start()

        @pl.when(gz < last)
        def _():
            rs_b[k] = right.astype(BF16)
            remote(
                rs_b.at[k], p1b.at[sweep, gz, gy], S_B1 + sweep, R_B1 + sweep,
                along_col(last - gz, 0),
            ).start()

        @pl.when(gy == last)
        def _():
            own_a[gz] = left

        @pl.when(gz == last)
        def _():
            own_b[gy] = right

        @pl.when(jnp.logical_and(gy == last - 1, gz > 0))
        def _():
            g = gz - 1
            rs2a[g] = finish_a(sweep, g).astype(BF16)
            remote(
                rs2a.at[g], p2a.at[sweep, g], S_A2 + sweep, R_A2 + sweep, along_col(last - g, 0)
            ).start()

    for sweep in range(n_sweeps):
        charges_of(sweep)

        def close_b():
            wait_for(p1b.at[sweep], S_B1 + sweep, R_B1 + sweep).wait_recv()
            for g in range(last):
                rs2b[g] = finish_b(sweep, g).astype(BF16)
                remote(
                    rs2b.at[g], p2b.at[sweep, g], S_B2 + sweep, R_B2 + sweep, along_col(0, last - g)
                ).start()

        def upper(k, carry):
            value = jnp.dot(tile_a[part(k, tri), :], qq[...], preferred_element_type=F32)
            emit(sweep, k, value)
            return carry

        def lower(k, carry, more):
            value = jnp.dot(tile_b[part(k - n_a, tri), :], qq[...], preferred_element_type=F32)
            if more:
                make_tile(tile_b, k + 1, n_a)
            emit(sweep, k, value)
            return carry

        if sweep == 0:
            lax.fori_loop(0, n_a, upper, 0)
            make_tile(tile_b, n_a, n_a)
            lax.fori_loop(n_a, n_col - 1, functools.partial(lower, more=True), 0)
            close_b()
            lower(n_col - 1, 0, False)
        else:
            lax.fori_loop(0, n_a, upper, 0)
            lax.fori_loop(n_a, n_col, functools.partial(lower, more=False), 0)
            close_b()

        def answer(c):
            def one(h):
                at = part(h, chunk)
                f_out[c, at, :] = jnp.dot(pick[at, :], pot[c], preferred_element_type=F32).astype(BF16)
                for j in first_of(h):
                    d = h * group + j
                    remote(
                        f_out.at[c, block(d)], f_in.at[sweep, c, block(d)],
                        S_F + 2 * sweep + c, R_F + 2 * sweep + c, behind(d),
                    ).start()

            all_chunks(one)
            f_in[sweep, c, 0:slots, :] = f_out[c, 0:slots, :]
            if sweep == n_sweeps - 1:
                pot_ref[:, c * half:(c + 1) * half] = pot[c]

        left = finish_a(sweep, last)
        wait_for(p2a.at[sweep], S_A2 + sweep, R_A2 + sweep).wait_recv()
        for j in range(last):
            left = left + p2a[sweep, j].astype(F32)
        pot[0] = left.astype(BF16)
        answer(0)
        right = finish_b(sweep, last)
        wait_for(p2b.at[sweep], S_B2 + sweep, R_B2 + sweep).wait_recv()
        for j in range(last):
            right = right + p2b[sweep, j].astype(F32)
        pot[1] = right.astype(BF16)
        answer(1)
        wait_for(rs_a.at[pl.ds(0, last * side)], S_A1 + sweep, R_B1 + sweep).wait_send()
        wait_for(rs_b.at[pl.ds(0, last * side)], S_B1 + sweep, R_B1 + sweep).wait_send()
        wait_for(rs2a, S_A2 + sweep, R_A2 + sweep).wait_send()
        wait_for(rs2b, S_B2 + sweep, R_B2 + sweep).wait_send()
        for c in range(2):
            at = 2 * sweep + c
            f_wait = remote(f_out.at[c, rest], f_in.at[sweep, c, rest], S_F + at, R_F + at, nobody)
            f_wait.wait_recv()
            slope = jnp.dot(place_t[...], f_in[sweep, c], preferred_element_type=F32)
            updated = (cur[c].astype(F32) - w_ref[sweep] * slope).astype(BF16)
            if sweep == n_sweeps - 1:
                upd_ref[:, c * half:(c + 1) * half] = updated
            else:
                cur[c] = updated

                def next_out(h):
                    fill_out(c, h)
                    send_out(sweep + 1, c, h)

                all_chunks(next_out)
                b_in[sweep + 1, c, 0:slots, :] = b_out[c, 0:slots, :]
            f_wait.wait_send()


def solution(mesh):
    n_row, n_col = mesh.shape["row"], mesh.shape["col"]
    devices = n_row * n_col

    def per_device(currents, incidence, centroids, sweep_weights):
        edge_dev, width = currents.shape
        tri = centroids.shape[1]
        n_sweeps = sweep_weights.shape[0]
        slots = 16
        cells = devices * slots
        vm = pltpu.VMEM
        return pl.pallas_call(
            functools.partial(kernel, n_row, n_col),
            out_shape=(
                jax.ShapeDtypeStruct((edge_dev, width), BF16),
                jax.ShapeDtypeStruct((tri, width), BF16),
            ),
            in_specs=[pl.BlockSpec(memory_space=pltpu.VMEM)] * 3
            + [pl.BlockSpec(memory_space=pltpu.SMEM)],
            out_specs=(pl.BlockSpec(memory_space=pltpu.VMEM),) * 2,
            scratch_shapes=[
                vm((n_col * tri // 2, 2 * n_row * tri), BF16),
                vm((n_col * tri // 2, 2 * n_row * tri), BF16),
                vm((2, cells, width // 2), BF16),
                vm((n_sweeps, 2, cells, width // 2), BF16),
                vm((2, cells, width // 2), BF16),
                vm((n_sweeps, 2, cells, width // 2), BF16),
                vm((n_sweeps, 2, n_row * tri, width // 2), BF16),
                vm((2 * n_row * tri, width), BF16),
                vm((cells, edge_dev), BF16),
                vm((edge_dev, cells), BF16),
                vm((cells, tri), BF16),
                vm((tri, cells), BF16),
                vm((n_col, tri, width // 2), BF16),
                vm((n_col, tri, width // 2), BF16),
                vm((4, tri, width // 2), F32),
                vm((4, tri, width // 2), F32),
                vm((n_sweeps, 4, 3, tri, width // 2), BF16),
                vm((n_sweeps, 3, 4, tri, width // 2), BF16),
                vm((3, tri, width // 2), BF16),
                vm((3, tri, width // 2), BF16),
                vm((n_sweeps, 3, tri, width // 2), BF16),
                vm((n_sweeps, 3, tri, width // 2), BF16),
                vm((devices, 128), F32),
                vm((devices, 1, 128), F32),
                vm((devices, 1, 128), F32),
                vm((n_col, 3, tri), jnp.int32),
                vm((n_row, 3, tri), jnp.int32),
                vm((16, n_col * tri), BF16),
                vm((16, n_row * tri), BF16),
                vm((2, edge_dev, width // 2), BF16),
                vm((2, tri, width // 2), BF16),
                pltpu.SemaphoreType.DMA((3 + 10 * n_sweeps,)),
                pltpu.SemaphoreType.DMA((3 + 21 * n_sweeps,)),
            ],
            compiler_params=pltpu.CompilerParams(
                collective_id=0, has_side_effects=True, vmem_limit_bytes=66000000
            ),
            name="sweeps",
        )(currents, incidence, centroids, sweep_weights)

    in_specs = (P(("row", "col"), None), P(None, ("row", "col")), P(None, ("row", "col")), P())
    out_specs = (P(("row", "col"), None), P(("row", "col"), None))
    return jax.shard_map(
        per_device, mesh=mesh, in_specs=in_specs, out_specs=out_specs, check_vma=False
    )
```

```python
import functools

import jax
import jax.numpy as jnp
from jax import lax
from jax.experimental import pallas as pl
from jax.experimental.pallas import tpu as pltpu
from jax.sharding import PartitionSpec as P

MESH = pl.DeviceIdType.MESH
F32 = jnp.float32
BF16 = jnp.bfloat16

AMP = 0.2 / 32.0
ROOT = (2.0 * AMP) ** 0.5
SIN = (3.14158202, -5.1671428, 2.54189902, -0.554636165)
COS = (-0.11181640625, 0.55078125, -0.4453125, 0.1328125)


def iota(shape, dim):
    return lax.broadcasted_iota(jnp.int32, shape, dim)


def horner(coefs, s, scale):
    acc = jnp.float32(coefs[-1] * scale)
    for c in coefs[-2::-1]:
        acc = acc * s + jnp.float32(c * scale)
    return acc


def horner16(coefs, s):
    acc = BF16(coefs[-1])
    for c in coefs[-2::-1]:
        acc = acc * s + BF16(c)
    return acc


def features(points, as_rows):
    n = points.shape[1]
    x, y, z = points[0:1], points[1:2], points[2:3]
    norm = x * x + y * y + z * z
    if as_rows:
        norm = norm + 1
    top = norm - (norm & 511)
    low = norm & 511
    mid = low - (low & 1)
    bit = low & 1
    one = jnp.ones((1, n), jnp.int32)
    if as_rows:
        rows = [x, y, z, top, mid, bit, one, one, one]
        scale = 1.0
    else:
        rows = [-2 * x, -2 * y, -2 * z, one, one, one, top, mid, bit]
        scale = 1.0 / 1024.0
    at = iota((16, n), 0)
    out = jnp.zeros((16, n), F32)
    for k, row in enumerate(rows):
        out = jnp.where(at == k, row.astype(F32) * scale, out)
    return out.astype(BF16)


def kernel(
    n_row, n_col,
    cur_ref, inc_ref, cen_ref, w_ref,
    upd_ref, pot_ref,
    tile_a, tile_b, b_out, b_in, f_out, f_in, q_in, qq, place, place_t, pick, pick_t,
    rs_a, rs_b, own_a, own_b, p1a, p1b, rs2a, rs2b, p2a, p2b,
    lab_flat, lab_out, lab_in, row_cen, col_cen, feat_row, feat_col, cur, pot,
    send_sem, recv_sem,
):
    devices = n_row * n_col
    edge_dev, width = cur_ref.shape
    half = width // 2
    tri = cen_ref.shape[1]
    cells = b_out.shape[1]
    slots = cells // devices
    n_cols = n_row * tri
    n_sweeps = w_ref.shape[0]
    side = 4
    my_row, my_col = lax.axis_index("row"), lax.axis_index("col")
    me = my_row * n_col + my_col
    mx, mc = lax.div(my_row, 2), lax.rem(my_row, 2)
    mz, my = lax.div(my_col, side), lax.rem(my_col, side)

    def flat_id(index):
        return (lax.div(index, n_col), lax.rem(index, n_col))

    def ahead(d):
        return flat_id(lax.rem(me + d, devices))

    def behind(d):
        return flat_id(lax.rem(me + devices - d, devices))

    def along_row(dx, dc):
        return (lax.rem(mx + dx, side) * 2 + lax.rem(mc + dc, 2), my_col)

    def along_col(dz, dy):
        return (my_row, lax.rem(mz + dz, side) * side + lax.rem(my + dy, side))

    sends, recvs = [0], [0]

    def new(count, many):
        count[0] += many
        return count[0] - many

    S_ROWC, S_COLC, S_LAB = (new(sends, 1) for _ in range(3))
    R_ROWC, R_COLC, R_LAB = (new(recvs, 1) for _ in range(3))
    S_A1, S_B1, S_A2, S_B2 = (new(sends, n_sweeps) for _ in range(4))
    S_B, S_Q, S_F = (new(sends, 2 * n_sweeps) for _ in range(3))
    R_B1, R_A2, R_B2 = (new(recvs, n_sweeps) for _ in range(3))
    R_B, R_Q2, R_F = (new(recvs, 2 * n_sweeps) for _ in range(3))
    R_A1 = new(recvs, n_sweeps * side)
    R_Q1 = new(recvs, 2 * n_sweeps * side)

    def remote(src, dst, s, r, device):
        return pltpu.make_async_remote_copy(
            src_ref=src, dst_ref=dst, send_sem=send_sem.at[s], recv_sem=recv_sem.at[r],
            device_id=device, device_id_type=MESH,
        )

    barrier = pltpu.get_barrier_semaphore()

    def greet(h, carry):
        for j in range(8):
            d = devices - 1 - h * 8 - j
            pl.semaphore_signal(barrier, inc=1, device_id=ahead(d), device_id_type=MESH)
        return carry

    lax.fori_loop(0, devices // 8 - 1, greet, 0)
    for d in range(1, 8):
        pl.semaphore_signal(barrier, inc=1, device_id=ahead(d), device_id_type=MESH)

    both = jnp.concatenate([inc_ref[0:1, :], inc_ref[1:2, :]], axis=1)
    n_con = both.shape[1]
    owner = lax.shift_right_logical(both, tri.bit_length() - 1)
    local = (both & (tri - 1)).astype(F32)
    rel = (owner - me + devices) & (devices - 1)
    hits = jnp.where(rel == iota((devices, n_con), 0), 1.0, 0.0)
    hits16 = hits.astype(BF16)
    earlier = jnp.where(iota((n_con, n_con), 0) < iota((n_con, n_con), 1), 1.0, 0.0).astype(BF16)
    before = jnp.dot(hits16, earlier, preferred_element_type=F32)
    rank = jnp.sum(hits * before, axis=0, keepdims=True)
    slot = rel.astype(F32) * float(slots) + rank
    marks = jnp.where(rank == iota((128, n_con), 0).astype(F32), local + 1.0, 0.0).astype(BF16)
    lab_flat[...] = lax.dot_general(
        hits16, marks, (((1,), (1,)), ((), ())), preferred_element_type=F32
    )
    slot_plus, slot_minus = slot[:, :edge_dev], slot[:, edge_dev:]

    def spread(d, carry):
        lab_out[d] = lab_flat[pl.ds(d, 1), :]
        return carry

    lax.fori_loop(0, devices, spread, 0)
    chunk = 256
    group = chunk // slots
    for c in range(2):
        cur[c] = cur_ref[:, c * half:(c + 1) * half]

    def part(h, size):
        return pl.ds(h * size if isinstance(h, int) else pl.multiple_of(h * size, size), size)

    def block(d):
        return part(d, slots)

    rest = pl.ds(slots, cells - slots)
    nobody = ahead(1)

    def fill_place(h, carry):
        at = (iota((chunk, edge_dev), 0) + h * chunk).astype(F32)
        rows = jnp.where(slot_plus == at, 1.0, 0.0) - jnp.where(slot_minus == at, 1.0, 0.0)
        place[part(h, chunk), :] = rows.astype(BF16)
        place_t[:, part(h, chunk)] = rows.T.astype(BF16)
        return carry

    lax.fori_loop(0, cells // chunk, fill_place, 0)

    def fill_out(c, h):
        at = part(h, chunk)
        b_out[c, at, :] = jnp.dot(place[at, :], cur[c], preferred_element_type=F32).astype(BF16)

    def first_of(h):
        return range(1 if isinstance(h, int) else 0, group)

    def send_out(sweep, c, h):
        for j in first_of(h):
            d = h * group + j
            remote(
                b_out.at[c, block(d)], b_in.at[sweep, c, block(d)],
                S_B + 2 * sweep + c, R_B + 2 * sweep + c, ahead(d),
            ).start()

    def all_chunks(one):
        one(0)

        def other(h, carry):
            one(h)
            return carry

        lax.fori_loop(1, cells // chunk, other, 0)

    def fill_first(h, carry):
        fill_out(0, h)
        fill_out(1, h)
        return carry

    lax.fori_loop(0, cells // chunk, fill_first, 0)
    pl.semaphore_wait(barrier, devices - 1)

    def send_row_cen(k, carry):
        to = along_col(lax.div(k, side) + 1, lax.rem(k, side) + 1)
        remote(cen_ref, row_cen.at[k], S_ROWC, R_ROWC, to).start()
        return carry

    def send_col_cen(r, carry):
        to = along_row(lax.rem(r, side), lax.div(r, side))
        remote(cen_ref, col_cen.at[r], S_COLC, R_COLC, to).start()
        return carry

    lax.fori_loop(1, n_row, send_col_cen, 0)
    lax.fori_loop(0, n_col - 1, send_row_cen, 0)

    def send_labels(h):
        for j in first_of(h):
            d = h * group + j
            remote(lab_out.at[d], lab_in.at[d], S_LAB, R_LAB, ahead(d)).start()

    def send_first(h):
        for j in first_of(h):
            d = h * group + j
            remote(b_out.at[:, block(d)], b_in.at[0, :, block(d)], S_B, R_B, ahead(d)).start()

    all_chunks(send_labels)
    all_chunks(send_first)
    b_in[0, :, 0:slots, :] = b_out[:, 0:slots, :]
    lab_in[0] = lab_out[0]
    row_cen[n_col - 1] = cen_ref[...]
    col_cen[0] = cen_ref[...]

    drop_rows = pl.ds(0, n_col - 1)
    drop_cols = pl.ds(1, n_row - 1)
    row_wait = remote(row_cen.at[drop_rows], row_cen.at[drop_rows], S_ROWC, R_ROWC, nobody)
    col_wait = remote(col_cen.at[drop_cols], col_cen.at[drop_cols], S_COLC, R_COLC, nobody)
    col_wait.wait_send()
    col_wait.wait_recv()
    for r in range(n_row):
        feat_col[:, r * tri:(r + 1) * tri] = features(col_cen[r], False)
    row_wait.wait_send()
    row_wait.wait_recv()
    for t in range(n_col):
        feat_row[:, t * tri:(t + 1) * tri] = features(row_cen[t], True)

    step = 128

    def make_tile(tile, k, base):
        for u in range(tri // step):
            at, here = part(k * (tri // step) + u, step), part((k - base) * (tri // step) + u, step)
            dist = lax.dot_general(
                feat_row[:, at], feat_col[...], (((0,), (0,)), ((), ())), preferred_element_type=F32
            )
            inv = lax.rsqrt(dist)
            turns = dist * inv
            r = turns - jnp.round(turns)
            s = r * r
            sine = r * horner(SIN, s, ROOT)
            cosine = horner16(COS, s.astype(BF16))
            tile[here, 0:n_cols] = (inv * (jnp.float32(AMP) - sine * sine)).astype(BF16)
            tile[here, n_cols:2 * n_cols] = (inv * sine).astype(BF16) * cosine

    def make_a(k, carry):
        make_tile(tile_a, k, 0)
        return carry

    n_a = tile_a.shape[0] // tri
    cuts = (0, 5, 6, 7, 8, n_a)

    def more_tile(stage):
        lax.fori_loop(cuts[stage], cuts[stage + 1], make_a, 0)

    def fill_qq(sweep, c, r):
        at = pl.ds(r * tri, tri)
        below = pl.ds(n_cols + r * tri, tri)
        q = q_in[sweep, c, at, :]
        if c == 0:
            qq[at, :half] = q
            qq[below, half:] = q
        else:
            qq[at, half:] = q
            qq[below, :half] = -q

    def read_labels():
        labels = remote(
            lab_out.at[pl.ds(1, devices - 1)], lab_in.at[pl.ds(1, devices - 1)], S_LAB, R_LAB, nobody
        )
        labels.wait_send()
        labels.wait_recv()

        def gather(d, carry):
            lab_flat[pl.ds(d, 1), :] = lab_in[d]
            return carry

        lax.fori_loop(0, devices, gather, 0)
        widen = jnp.where(
            lax.div(iota((chunk, group), 0), slots) == iota((chunk, group), 1), 1.0, 0.0
        ).astype(BF16)
        keep = jnp.where(
            lax.rem(iota((chunk, 128), 0), slots) == iota((chunk, 128), 1), 1.0, 0.0
        )
        ones = jnp.ones((128, tri), BF16)
        target = (iota((chunk, tri), 1) + 1).astype(F32)

        def fill_pick(h, carry):
            here = lab_flat[part(h, group), :].astype(BF16)
            wide = jnp.dot(widen, here, preferred_element_type=F32) * keep
            label = jnp.dot(wide.astype(BF16), ones, preferred_element_type=F32)
            rows = jnp.where(label == target, 1.0, 0.0)
            pick[part(h, chunk), :] = rows.astype(BF16)
            pick_t[:, part(h, chunk)] = rows.T.astype(BF16)
            return carry

        lax.fori_loop(0, cells // chunk, fill_pick, 0)

    def charges_of(sweep):
        partner = along_row(0, 1)
        waits = []
        if sweep == 0:
            more_tile(0)
            read_labels()
        for c in range(2):
            at = 2 * sweep + c
            if sweep > 0:
                wait = remote(b_out.at[c, rest], b_in.at[sweep, c, rest], S_B + at, R_B + at, nobody)
                wait.wait_recv()
                waits.append(wait)
            elif c == 0:
                wait = remote(b_out.at[:, rest], b_in.at[0, :, rest], S_B, R_B, nobody)
                wait.wait_recv()
                waits.append(wait)
            q_in[sweep, c, 0:tri, :] = jnp.dot(
                pick_t[...], b_in[sweep, c], preferred_element_type=F32
            ).astype(BF16)
            mine = q_in.at[sweep, c, pl.ds(0, tri)]
            for dx in (2, 1, 3):
                remote(
                    mine, q_in.at[sweep, c, pl.ds(dx * tri, tri)],
                    S_Q + at, R_Q1 + at * side + dx, along_row(dx, 0),
                ).start()
            remote(mine, q_in.at[sweep, c, pl.ds(side * tri, tri)], S_Q + at, R_Q2 + at, partner).start()
            fill_qq(sweep, c, 0)
            if sweep == 0 and c == 1:
                more_tile(1)
                more_tile(2)
        for c in range(2):
            at = 2 * sweep + c
            for dx in (1, 3, 2):
                got = q_in.at[sweep, c, pl.ds(dx * tri, tri)]
                remote(got, got, S_Q + at, R_Q1 + at * side + dx, partner).wait_recv()
                remote(
                    got, q_in.at[sweep, c, pl.ds((side + dx) * tri, tri)], S_Q + at, R_Q2 + at, partner
                ).start()
                fill_qq(sweep, c, dx)
            if sweep == 0:
                more_tile(3 + c)
        for c in range(2):
            at = 2 * sweep + c
            far = q_in.at[sweep, c, pl.ds(side * tri, side * tri)]
            remote(far, far, S_Q + at, R_Q2 + at, nobody).wait_recv()
            for r in range(side, 2 * side):
                fill_qq(sweep, c, r)
            if c < len(waits):
                waits[c].wait_send()
            sent = q_in.at[sweep, c, pl.ds(tri, n_cols - tri)]
            remote(sent, sent, S_Q + at, R_Q2 + at, nobody).wait_send()

    def wait_for(ref, s, r):
        return remote(ref, ref, s, r, nobody)

    last = side - 1

    def finish_a(sweep, g):
        wait_for(p1a.at[sweep, g], S_A1 + sweep, R_A1 + sweep * side + g).wait_recv()
        total = own_a[g]
        for j in range(last):
            total = total + p1a[sweep, g, j].astype(F32)
        return total

    def finish_b(sweep, g):
        total = own_b[g]
        for j in range(last):
            total = total + p1b[sweep, j, g].astype(F32)
        return total

    def emit(sweep, k, value):
        k = jnp.int32(k)
        gz, gy = lax.div(k, side), lax.rem(k, side)
        left, right = value[:, :half], value[:, half:]

        @pl.when(gy < last)
        def _():
            rs_a[k] = left.astype(BF16)
            remote(
                rs_a.at[k], p1a.at[sweep, gz, gy], S_A1 + sweep, R_A1 + sweep * side + gz,
                along_col(0, last - gy),
            ).start()

        @pl.when(gz < last)
        def _():
            rs_b[k] = right.astype(BF16)
            remote(
                rs_b.at[k], p1b.at[sweep, gz, gy], S_B1 + sweep, R_B1 + sweep,
                along_col(last - gz, 0),
            ).start()

        @pl.when(gy == last)
        def _():
            own_a[gz] = left

        @pl.when(gz == last)
        def _():
            own_b[gy] = right

        def close_a(g):
            rs2a[g] = finish_a(sweep, g).astype(BF16)
            remote(
                rs2a.at[g], p2a.at[sweep, g], S_A2 + sweep, R_A2 + sweep, along_col(last - g, 0)
            ).start()

        if sweep == 0:
            @pl.when(jnp.logical_and(gy == last - 1, gz > 0))
            def _():
                close_a(gz - 1)
        else:
            @pl.when(jnp.logical_and(gz == last, gy < last))
            def _():
                close_a(gy)

    for sweep in range(n_sweeps):
        charges_of(sweep)

        def close_b():
            wait_for(p1b.at[sweep], S_B1 + sweep, R_B1 + sweep).wait_recv()
            for g in range(last):
                rs2b[g] = finish_b(sweep, g).astype(BF16)
                remote(
                    rs2b.at[g], p2b.at[sweep, g], S_B2 + sweep, R_B2 + sweep, along_col(0, last - g)
                ).start()

        def upper(k, carry):
            value = jnp.dot(tile_a[part(k, tri), :], qq[...], preferred_element_type=F32)
            emit(sweep, k, value)
            return carry

        def lower(k, carry, more):
            value = jnp.dot(tile_b[part(k - n_a, tri), :], qq[...], preferred_element_type=F32)
            if more:
                make_tile(tile_b, k + 1, n_a)
            emit(sweep, k, value)
            return carry

        if sweep == 0:
            lax.fori_loop(0, n_a, upper, 0)
            make_tile(tile_b, n_a, n_a)
            lax.fori_loop(n_a, n_col - 1, functools.partial(lower, more=True), 0)
            close_b()
            lower(n_col - 1, 0, False)
        else:
            lax.fori_loop(0, n_a, upper, 0)
            lax.fori_loop(n_a, n_col, functools.partial(lower, more=False), 0)
            close_b()

        def answer(c):
            def one(h):
                at = part(h, chunk)
                f_out[c, at, :] = jnp.dot(pick[at, :], pot[c], preferred_element_type=F32).astype(BF16)
                for j in first_of(h):
                    d = h * group + j
                    remote(
                        f_out.at[c, block(d)], f_in.at[sweep, c, block(d)],
                        S_F + 2 * sweep + c, R_F + 2 * sweep + c, behind(d),
                    ).start()

            all_chunks(one)
            f_in[sweep, c, 0:slots, :] = f_out[c, 0:slots, :]
            if sweep == n_sweeps - 1:
                pot_ref[:, c * half:(c + 1) * half] = pot[c]

        left = finish_a(sweep, last)
        wait_for(p2a.at[sweep], S_A2 + sweep, R_A2 + sweep).wait_recv()
        for j in range(last):
            left = left + p2a[sweep, j].astype(F32)
        pot[0] = left.astype(BF16)
        answer(0)
        right = finish_b(sweep, last)
        wait_for(p2b.at[sweep], S_B2 + sweep, R_B2 + sweep).wait_recv()
        for j in range(last):
            right = right + p2b[sweep, j].astype(F32)
        pot[1] = right.astype(BF16)
        answer(1)
        wait_for(rs_a.at[pl.ds(0, last * side)], S_A1 + sweep, R_B1 + sweep).wait_send()
        wait_for(rs_b.at[pl.ds(0, last * side)], S_B1 + sweep, R_B1 + sweep).wait_send()
        wait_for(rs2a, S_A2 + sweep, R_A2 + sweep).wait_send()
        wait_for(rs2b, S_B2 + sweep, R_B2 + sweep).wait_send()
        for c in range(2):
            at = 2 * sweep + c
            f_wait = remote(f_out.at[c, rest], f_in.at[sweep, c, rest], S_F + at, R_F + at, nobody)
            f_wait.wait_recv()
            slope = jnp.dot(place_t[...], f_in[sweep, c], preferred_element_type=F32)
            updated = (cur[c].astype(F32) - w_ref[sweep] * slope).astype(BF16)
            if sweep == n_sweeps - 1:
                upd_ref[:, c * half:(c + 1) * half] = updated
            else:
                cur[c] = updated

                def next_out(h):
                    fill_out(c, h)
                    send_out(sweep + 1, c, h)

                all_chunks(next_out)
                b_in[sweep + 1, c, 0:slots, :] = b_out[c, 0:slots, :]
            f_wait.wait_send()


def solution(mesh):
    n_row, n_col = mesh.shape["row"], mesh.shape["col"]
    devices = n_row * n_col

    def per_device(currents, incidence, centroids, sweep_weights):
        edge_dev, width = currents.shape
        tri = centroids.shape[1]
        n_sweeps = sweep_weights.shape[0]
        slots = 16
        cells = devices * slots
        vm = pltpu.VMEM
        return pl.pallas_call(
            functools.partial(kernel, n_row, n_col),
            out_shape=(
                jax.ShapeDtypeStruct((edge_dev, width), BF16),
                jax.ShapeDtypeStruct((tri, width), BF16),
            ),
            in_specs=[pl.BlockSpec(memory_space=pltpu.VMEM)] * 3
            + [pl.BlockSpec(memory_space=pltpu.SMEM)],
            out_specs=(pl.BlockSpec(memory_space=pltpu.VMEM),) * 2,
            scratch_shapes=[
                vm((9 * tri, 2 * n_row * tri), BF16),
                vm(((n_col - 9) * tri, 2 * n_row * tri), BF16),
                vm((2, cells, width // 2), BF16),
                vm((n_sweeps, 2, cells, width // 2), BF16),
                vm((2, cells, width // 2), BF16),
                vm((n_sweeps, 2, cells, width // 2), BF16),
                vm((n_sweeps, 2, n_row * tri, width // 2), BF16),
                vm((2 * n_row * tri, width), BF16),
                vm((cells, edge_dev), BF16),
                vm((edge_dev, cells), BF16),
                vm((cells, tri), BF16),
                vm((tri, cells), BF16),
                vm((n_col, tri, width // 2), BF16),
                vm((n_col, tri, width // 2), BF16),
                vm((4, tri, width // 2), F32),
                vm((4, tri, width // 2), F32),
                vm((n_sweeps, 4, 3, tri, width // 2), BF16),
                vm((n_sweeps, 3, 4, tri, width // 2), BF16),
                vm((3, tri, width // 2), BF16),
                vm((3, tri, width // 2), BF16),
                vm((n_sweeps, 3, tri, width // 2), BF16),
                vm((n_sweeps, 3, tri, width // 2), BF16),
                vm((devices, 128), F32),
                vm((devices, 1, 128), F32),
                vm((devices, 1, 128), F32),
                vm((n_col, 3, tri), jnp.int32),
                vm((n_row, 3, tri), jnp.int32),
                vm((16, n_col * tri), BF16),
                vm((16, n_row * tri), BF16),
                vm((2, edge_dev, width // 2), BF16),
                vm((2, tri, width // 2), BF16),
                pltpu.SemaphoreType.DMA((3 + 10 * n_sweeps,)),
                pltpu.SemaphoreType.DMA((3 + 21 * n_sweeps,)),
            ],
            compiler_params=pltpu.CompilerParams(
                collective_id=0, has_side_effects=True, vmem_limit_bytes=66000000
            ),
            name="sweeps",
        )(currents, incidence, centroids, sweep_weights)

    in_specs = (P(("row", "col"), None), P(None, ("row", "col")), P(None, ("row", "col")), P())
    out_specs = (P(("row", "col"), None), P(("row", "col"), None))
    return jax.shard_map(
        per_device, mesh=mesh, in_specs=in_specs, out_specs=out_specs, check_vma=False
    )
```
